512 devices in a mesh: gx: 32 (over z, x), gy: 16 (over y, core).
Axes of the slice: x: 4, y: 8, z: 8, core: 2. Of those that a mesh axis runs over, the one named last changes fastest.
Arguments:
- eigen: float32 [256, 256, 256], P('gx', 'gy'), may hold values from -6 to 6
- seg_vec: float32 [6, 32, 16, 2048], P(None, 'gx', 'gy'), may hold values from -5 to 5
- seg_off: float32 [3, 32, 16, 2048], P(None, 'gx', 'gy'), may hold values from 0 to 1
- seg_cell: int32 [32, 16, 2048], P('gx', 'gy'), may hold values from 0 to 32767
- blk_count: int32 [32, 16, 16], P('gx', 'gy'), may hold values from 0 to 128, as said below
- pair_list: int32 [32, 16, 16, 8], P('gx', 'gy'), may hold values from 0 to 143, as said below
Outputs:
- stress_field: float32 [256, 256, 256], P('gx', 'gy')
- seg_force: float32 [3, 32, 16, 2048], P(None, 'gx', 'gy')
The draws below stay inside these ranges and needn't reach their ends.
Inputs may be any that keep to these rules, and one draw needn't show every extreme that they name: `blk_count`: A block's live segments fill its first slots; at least one device holds 16 full blocks of 128; every device holds a block with segments. `pair_list`: the 8 entries of one block are distinct.
All inputs are finite; a program needn't handle non-finite values.
Results may differ from the reference program's by a relative error of at most 0.0003.
Values sent between devices are 32-bit elements; how exact they have to be, the bound alone decides.
A program may use at most 64 MiB of HBM per device.

```python
import math
import jax
import jax.numpy as jnp
from jax import lax

GRID = 256
SEGS_BLK = 128
BLK_DEV = 16
PARTNERS = 8
SEG_DEV = 2048
CELLS_DEV = 32768
N_GX = 32
N_GY = 16


def draw_eigen(key, part):
    first = jax.random.fold_in(key, 0)
    field = jax.random.normal(first, (GRID, GRID, GRID), jnp.float32)
    return jnp.clip(field, -6.0, 6.0)


def draw_blk_count(key, part):
    key_list = jax.random.split(key, 4)
    devices = N_GX * N_GY
    tangled = jax.random.randint(key_list[0], (devices,), 0, 8) == 0
    chosen = jax.random.randint(key_list[1], (), 0, devices)
    tangled = tangled | (jnp.arange(devices, dtype=jnp.int32) == chosen)
    live_blocks = jax.random.randint(key_list[2], (devices,), 1, max(BLK_DEV // 2, 1) + 1)
    live_blocks = jnp.where(tangled, BLK_DEV, live_blocks)
    filled = jax.random.randint(key_list[3], (devices, BLK_DEV), SEGS_BLK // 4, SEGS_BLK + 1)
    filled = jnp.where(tangled[:, None], SEGS_BLK, filled)
    result = jnp.where(jnp.arange(BLK_DEV, dtype=jnp.int32)[None, :] < live_blocks[:, None], filled, 0)
    return result.astype(jnp.int32).reshape(N_GX, N_GY, BLK_DEV)


def draw_pair_list(key, part):
    row_total = N_GX * N_GY * BLK_DEV
    pool_size = 9 * BLK_DEV
    scores = jax.random.randint(key, (row_total, pool_size), 0, 1 << 20)
    scores = scores * pool_size + jnp.arange(pool_size, dtype=jnp.int32)[None, :]
    ranking = jnp.argsort(scores, axis=1)
    return ranking[:, :PARTNERS].astype(jnp.int32).reshape(N_GX, N_GY, BLK_DEV, PARTNERS)


def touch_ends(entries, stream_key, smallest, largest):
    dims = entries.shape
    spot = [jax.random.randint(jax.random.fold_in(stream_key, axis), (), 0, dims[axis]) for axis in range(len(dims))]
    entries = entries.at[tuple(spot)].set(smallest)
    longest = dims.index(max(dims))
    spot[longest] = (spot[longest] + 1) % dims[longest]
    return entries.at[tuple(spot)].set(largest)


def steps_of(rng, extent, pieces, least, largest):
    level = 1.0
    for dim, shards_of in pieces:
        draws = jax.random.uniform(jax.random.fold_in(jax.random.fold_in(rng, 6), dim), (shards_of,), jnp.float32, least / len(pieces), largest / len(pieces))
        level = level * jnp.repeat(jnp.exp(draws), extent[dim] // shards_of).reshape((-1,) + (1,) * (len(extent) - 1 - dim))
    return level


def gaussian(own_key, shape, scale, bound, cuts=(), kind=jnp.bfloat16):
    values = scale * jax.random.normal(own_key, shape, jnp.float32)
    if cuts:
        values = values * steps_of(own_key, shape, cuts, -0.22, 0.18)
    return jnp.clip(values, -bound, bound).astype(kind)


def setup_inputs(seed: int = 0) -> dict:
    key_of = jax.random.split(jax.random.key(seed), 7)
    eigen = draw_eigen(jax.random.fold_in(key_of[6], 71), 0)
    seg_vec = gaussian(key_of[1], (6, N_GX, N_GY, SEG_DEV), 1.0, 5.0, ((1, 32), (2, 16)), jnp.float32)
    seg_off = jnp.clip(1.0 * jax.random.uniform(key_of[2], (3, N_GX, N_GY, SEG_DEV), jnp.float32) ** steps_of(key_of[2], (3, N_GX, N_GY, SEG_DEV), ((1, 32), (2, 16)), -0.2, 0.2), 0.0, 1.0)
    seg_cell = touch_ends(jax.random.randint(key_of[3], (N_GX, N_GY, SEG_DEV), 0, CELLS_DEV), jax.random.fold_in(key_of[3], 1), 0, CELLS_DEV - 1).astype(jnp.int32)
    blk_count = draw_blk_count(jax.random.fold_in(key_of[6], 71), 0)
    pair_list = draw_pair_list(jax.random.fold_in(key_of[6], 71), 0)
    return {"eigen": eigen, "seg_vec": seg_vec, "seg_off": seg_off, "seg_cell": seg_cell, "blk_count": blk_count, "pair_list": pair_list}


nu_copper = 0.34
core_sq = 4.0
pair_scale = 4.0

def wave_sq(freq, length):
    sine = 2.0 * jnp.sin(math.pi * freq.astype(jnp.float32) / length)
    return sine * sine

def multiplier(wave_x, wave_y, wave_z, anchor):
    total = wave_x + wave_y + wave_z
    safe = jnp.where(anchor, 1.0, total)
    return -2.0 * (1.0 - (wave_x + wave_z) / safe + 2.0 * wave_x * wave_z / ((1.0 - nu_copper) * safe * safe))

def block_force(own_data, far_data, tau_own):
    deltas = [own_data[k][:, None] - far_data[k][None, :] for k in range(3)]
    dist_sq = deltas[0] * deltas[0] + deltas[1] * deltas[1] + deltas[2] * deltas[2] + core_sq
    inverse = 1.0 / jnp.sqrt(dist_sq)
    inv_three = inverse * inverse * inverse
    inv_five = inv_three * inverse * inverse
    burg_dot = own_data[3][:, None] * far_data[3][None, :] + own_data[4][:, None] * far_data[4][None, :] + own_data[5][:, None] * far_data[5][None, :]
    line_dot = own_data[6][:, None] * far_data[6][None, :] + own_data[7][:, None] * far_data[7][None, :] + own_data[8][:, None] * far_data[8][None, :]
    burg_own = own_data[3][:, None] * deltas[0] + own_data[4][:, None] * deltas[1] + own_data[5][:, None] * deltas[2]
    burg_far = far_data[3][None, :] * deltas[0] + far_data[4][None, :] * deltas[1] + far_data[5][None, :] * deltas[2]
    weight = line_dot * (burg_dot * inv_three - 3.0 * burg_own * burg_far * inv_five)
    pair_pull = jnp.stack([lax.optimization_barrier(jnp.sum(weight * deltas[k], axis=1)) for k in range(3)])
    burgers = own_data[3:6]
    tangent = own_data[6:9]
    glide_dir = jnp.stack([burgers[1] * tangent[2] - burgers[2] * tangent[1], burgers[2] * tangent[0] - burgers[0] * tangent[2], burgers[0] * tangent[1] - burgers[1] * tangent[0]])
    return pair_scale * pair_pull + tau_own[None, :] * glide_dir

def reference(eigen, seg_vec, seg_off, seg_cell, blk_count, pair_list):
    freq = jnp.arange(GRID, dtype=jnp.int32)
    wave = wave_sq(freq, GRID)
    anchor = (freq[:, None, None] == 0) & (freq[None, :, None] == 0) & (freq[None, None, :] == 0)
    gain = multiplier(wave[:, None, None], wave[None, :, None], wave[None, None, :], anchor)
    stress = jnp.real(jnp.fft.ifftn(jnp.fft.fftn(eigen) * gain)).astype(jnp.float32)
    plane_x = GRID // N_GX
    plane_y = GRID // N_GY
    blocks = stress.reshape(N_GX, plane_x, N_GY, plane_y, GRID).transpose(0, 2, 1, 3, 4).reshape(N_GX, N_GY, plane_x * plane_y * GRID)
    sampled = jnp.take_along_axis(blocks, seg_cell, axis=2)
    coord_z = seg_cell % GRID
    coord_y = seg_cell // GRID % plane_y
    coord_x = seg_cell // (GRID * plane_y)
    position = jnp.stack([coord_x, coord_y, coord_z]).astype(jnp.float32) + seg_off
    live = (jnp.arange(SEGS_BLK, dtype=jnp.int32)[None, None, None, :] < blk_count[..., None]).reshape(N_GX, N_GY, SEG_DEV).astype(jnp.float32)
    source = jnp.concatenate([position, seg_vec[0:3] * live[None], seg_vec[3:6]], axis=0)
    shift = (jnp.arange(3, dtype=jnp.int32) - 1).astype(jnp.float32)

    def device(device_id):
        row_id = device_id // N_GY
        col_id = device_id % N_GY
        row_ids = ((row_id + jnp.arange(3, dtype=jnp.int32) - 1) % N_GX).astype(jnp.int32)
        col_ids = ((col_id + jnp.arange(3, dtype=jnp.int32) - 1) % N_GY).astype(jnp.int32)
        nearby = source[:, row_ids][:, :, col_ids]
        nearby = nearby.at[0].add(shift[:, None, None] * plane_x).at[1].add(shift[None, :, None] * plane_y)
        source_pool = nearby.reshape(9, 9 * BLK_DEV, SEGS_BLK)
        own_blocks = source[:, row_id, col_id].reshape(9, BLK_DEV, SEGS_BLK).transpose(1, 0, 2)
        tau_blocks = sampled[row_id, col_id].reshape(BLK_DEV, SEGS_BLK)

        def one_block(inputs):
            own_data, partner_ids, tau_own = inputs
            far_data = source_pool[:, partner_ids].reshape(9, -1)
            return block_force(own_data, far_data, tau_own)
        return lax.map(one_block, (own_blocks, pair_list[row_id, col_id], tau_blocks))
    forces = lax.map(device, jnp.arange(N_GX * N_GY, dtype=jnp.int32))
    seg_force = forces.reshape(N_GX, N_GY, BLK_DEV, 3, SEGS_BLK).transpose(3, 0, 1, 2, 4).reshape(3, N_GX, N_GY, SEG_DEV)
    return (stress, seg_force)
```

```python
import functools
import math

import jax
import jax.numpy as jnp
import ml_dtypes
import numpy as np
from jax import lax
from jax.experimental import pallas as pl
from jax.experimental.pallas import tpu as pltpu
from jax.sharding import PartitionSpec as P

nu_copper = 0.34
core_sq = 4.0
pair_scale = 4.0

MESH = pl.DeviceIdType.MESH
ROWS = 9
LANES = 128


def cas_table(length):
    steps = np.arange(length)
    angle = (steps[:, None] * steps[None, :] % length) * (2.0 * math.pi / length)
    table = np.cos(angle) + np.sin(angle)
    high = table.astype(ml_dtypes.bfloat16)
    low = (table - high.astype(np.float64)).astype(ml_dtypes.bfloat16)
    return np.stack([high, low])


def parts(x):
    high = x.astype(jnp.bfloat16)
    return high, (x - high.astype(jnp.float32)).astype(jnp.bfloat16)


def mm(a, b):
    return jnp.dot(a, b, preferred_element_type=jnp.float32)


def times_table(x, tab):
    high, low = parts(x)
    return mm(high, tab[0]) + (mm(low, tab[0]) + mm(high, tab[1]))


def table_times(tab, x):
    high, low = parts(x)
    return mm(tab[0], high) + (mm(tab[0], low) + mm(tab[1], high))


def swap_blocks(tiles, width):
    count = len(tiles)
    lane = lax.broadcasted_iota(jnp.int32, (8, LANES), 1) // width
    tiles = list(tiles)
    bit = 1
    while bit < count:
        keep = (lane & bit) == 0
        shift = bit * width
        for i in range(count):
            if i & bit:
                continue
            a, c = tiles[i], tiles[i | bit]
            tiles[i] = jnp.where(keep, a, pltpu.roll(c, shift, 1))
            tiles[i | bit] = jnp.where(keep, pltpu.roll(a, LANES - shift, 1), c)
        bit *= 2
    return tiles


def kernel(
    nx, ny, eigen_hbm, vec_hbm, off_hbm, cell_hbm, count_ref, pair_ref, tab_hbm,
    stress_hbm, force_hbm,
    eigen, vec, off, cell, tab, send1, recv1, send2, recv2, send3, recv3, send4, recv4,
    mid_a, mid_b, gain, source, pool, by_block, own_wide, far_wide, pull, hot, stress, force,
    load_sem, send_sem, recv_sem, store_sem,
):
    me_x = lax.axis_index("gx")
    me_y = lax.axis_index("gy")

    barrier = pltpu.get_barrier_semaphore()

    def greet_x(i, _):
        pl.semaphore_signal(barrier, inc=1, device_id={"gx": lax.rem(me_x + i, nx)}, device_id_type=MESH)
        return 0

    def greet_y(i, _):
        pl.semaphore_signal(barrier, inc=1, device_id={"gy": lax.rem(me_y + i, ny)}, device_id_type=MESH)
        return 0

    lax.fori_loop(1, nx, greet_x, 0)
    lax.fori_loop(1, ny, greet_y, 0)
    for dx in (-1, 1):
        for dy in (-1, 1):
            peer = {"gx": lax.rem(me_x + dx + nx, nx), "gy": lax.rem(me_y + dy + ny, ny)}
            pl.semaphore_signal(barrier, inc=1, device_id=peer, device_id_type=MESH)

    loads = [
        pltpu.make_async_copy(src, dst, load_sem.at[n])
        for n, (src, dst) in enumerate(
            (
                (eigen_hbm.at[:, pl.ds(0, LANES)], eigen.at[0]),
                (eigen_hbm.at[:, pl.ds(LANES, LANES)], eigen.at[1]),
                (tab_hbm, tab),
                (vec_hbm, vec),
                (off_hbm, off),
                (cell_hbm, cell),
            )
        )
    ]
    for load in loads:
        load.start()
    for load in loads[:3]:
        load.wait()

    lines = jnp.concatenate(
        [
            jnp.concatenate([eigen[h, pl.ds(y, 8, stride=16), :] for h in range(2)], axis=1)
            for y in range(16)
        ],
        axis=0,
    )
    zeta = times_table(lines, tab)
    for h in range(2):
        tiles = [zeta[y * 8 : y * 8 + 8, h * LANES : (h + 1) * LANES] for y in range(16)]
        for j, tile in enumerate(swap_blocks(tiles, 8)):
            send1[h * 16 + j] = tile

    pl.semaphore_wait(barrier, nx - 1 + ny - 1 + 4)

    def exchange(axis, me, count, send, recv, stage):
        def push(i, _):
            peer = lax.rem(me + i, count)
            pltpu.make_async_remote_copy(
                src_ref=send.at[peer], dst_ref=recv.at[me], send_sem=send_sem.at[stage],
                recv_sem=recv_sem.at[stage], device_id={axis: peer}, device_id_type=MESH,
            ).start()
            return 0

        lax.fori_loop(1, count, push, 0)
        recv[me] = send[me]

    def arrived(buffer, count, stage):
        whole = buffer.at[pl.ds(0, count)]
        pltpu.make_async_copy(whole, whole, recv_sem.at[stage]).wait()

    def left(buffer, count, stage):
        whole = buffer.at[pl.ds(0, count)]
        pltpu.make_async_copy(whole, whole, send_sem.at[stage]).wait()

    exchange("gx", me_x, nx, send1, recv1, 0)

    for load in loads[3:]:
        load.wait()
    row_id = lax.broadcasted_iota(jnp.int32, (16, LANES), 0)
    lane_id = lax.broadcasted_iota(jnp.int32, (16, LANES), 1)
    counts = jnp.zeros((16, LANES), jnp.int32)
    for b in range(16):
        counts = jnp.where(row_id == b, count_ref[b], counts)
    live = jnp.where(lane_id < counts, 1.0, 0.0)
    place = cell[...]
    spots = (place >> 12, (place >> 8) & 15, place & 255)
    for k in range(3):
        source[k] = spots[k].astype(jnp.float32) + off[k]
        source[3 + k] = vec[k] * live
        source[6 + k] = vec[3 + k]
    for dx in (-1, 0, 1):
        for dy in (-1, 0, 1):
            if dx == 0 and dy == 0:
                continue
            peer = {"gx": lax.rem(me_x + dx + nx, nx), "gy": lax.rem(me_y + dy + ny, ny)}
            pltpu.make_async_remote_copy(
                src_ref=source, dst_ref=pool.at[(1 - dx) * 3 + (1 - dy)], send_sem=send_sem.at[4],
                recv_sem=recv_sem.at[4], device_id=peer, device_id_type=MESH,
            ).start()
    for r in range(ROWS):
        pool[4, r] = source[r]

    for r in range(ROWS):
        rows = source[r]
        for b in range(16):
            by_block[b, pl.ds(r, 1), :] = rows[b : b + 1]

    def wave(index):
        sine = 2.0 * jnp.sin(index.astype(jnp.float32) * (math.pi / 256.0))
        return sine * sine

    lane_row = lax.broadcasted_iota(jnp.int32, (8, LANES), 1)
    freq_z = me_x * 8 + (lane_row >> 4)
    freq_x = me_y * 16 + (lane_row & 15)
    wave_x, wave_z = wave(freq_x), wave(freq_z)
    both = wave_x + wave_z
    product = 2.0 / (1.0 - nu_copper) * wave_x * wave_z
    corner = (freq_x == 0) & (freq_z == 0)

    def fill_gain(i, _):
        freq_y = i * 8 + lax.broadcasted_iota(jnp.int32, (8, LANES), 0)
        total = both + wave(freq_y)
        safe = jnp.where(corner & (freq_y == 0), 1.0, total)
        inverse = 1.0 / safe
        gain[pl.ds(pl.multiple_of(i * 8, 8), 8), :] = (-2.0 / 256.0**3) * (
            1.0 - both * inverse + product * inverse * inverse
        )
        return 0

    lax.fori_loop(0, 32, fill_gain, 0)

    spot = ((place >> 7) & 1) * 128 + ((place >> 8) & 15) * 8 + (place >> 12)
    for b in range(16):
        want = jnp.broadcast_to(spot[b : b + 1], (256, LANES))
        at = lax.broadcasted_iota(jnp.int32, (256, LANES), 0)
        hot[:, b * LANES : (b + 1) * LANES] = jnp.where(want == at, 1.0, 0.0).astype(jnp.bfloat16)

    arrived(recv1, nx - 1, 0)
    held = recv1[...].reshape(256, LANES)
    along_x = times_table(held.T, tab)
    for h in range(2):
        mid_a[h] = along_x[:, h * LANES : (h + 1) * LANES]
    for h in range(2):
        for s in range(2):
            tiles = [mid_a[h, pl.ds(s * 64 + c, 8, stride=8), :] for c in range(8)]
            for j, tile in enumerate(swap_blocks(tiles, 16)):
                send2[h * 8 + j, s * 8 : s * 8 + 8, :] = tile
    exchange("gy", me_y, ny, send2, recv2, 1)

    arrived(pool, 8, 4)
    for p in range(3):
        for q in range(3):
            if p != 1:
                pool[p * 3 + q, 0] += (p - 1) * 8.0
            if q != 1:
                pool[p * 3 + q, 1] += (q - 1) * 16.0

    def pair_block(b, _):
        for n in range(8):
            partner = pair_ref[n, b]
            device = partner >> 4
            slot = partner & 15
            for r in range(ROWS):
                far_wide[n, r] = jnp.broadcast_to(pool[device, r, pl.ds(slot, 1), :], (8, LANES))
        columns = by_block[b].T
        for r in range(ROWS):
            own_wide[r] = jnp.broadcast_to(columns[:, r : r + 1], (LANES, LANES))

        def tile(i, _):
            rows = pl.ds(pl.multiple_of(i * 8, 8), 8)
            own = [own_wide[r, rows, :] for r in range(ROWS)]
            triple = [3.0 * own[3 + k] for k in range(3)]
            total = [jnp.zeros((8, LANES), jnp.float32) for _ in range(3)]
            for n in range(8):
                far = [far_wide[n, r] for r in range(ROWS)]
                delta = [own[k] - far[k] for k in range(3)]
                square = (delta[0] * delta[0] + core_sq) + (delta[1] * delta[1] + delta[2] * delta[2])
                inverse = lax.rsqrt(square)
                inv_two = inverse * inverse
                inv_three = inv_two * inverse
                burg_dot = own[3] * far[3] + own[4] * far[4] + own[5] * far[5]
                line_dot = own[6] * far[6] + own[7] * far[7] + own[8] * far[8]
                burg_own = triple[0] * delta[0] + triple[1] * delta[1] + triple[2] * delta[2]
                burg_far = far[3] * delta[0] + far[4] * delta[1] + far[5] * delta[2]
                weight = (line_dot * inv_three) * (burg_dot - (burg_own * burg_far) * inv_two)
                total = [total[k] + weight * delta[k] for k in range(3)]
            lane = lax.broadcasted_iota(jnp.int32, (8, LANES), 1)
            have = pull[rows, :]
            for k in range(3):
                have = jnp.where(lane == k * 16 + b, jnp.sum(total[k], axis=1, keepdims=True), have)
            pull[rows, :] = have
            return 0

        lax.fori_loop(0, 16, tile, 0)
        return 0

    pull[...] = jnp.zeros_like(pull)
    lax.fori_loop(0, 5, pair_block, 0)

    arrived(recv2, ny - 1, 1)
    spectrum = table_times(tab, recv2[...].reshape(256, LANES)) * gain[...]
    send3[...] = table_times(tab, spectrum).reshape(16, 16, LANES)
    exchange("gy", me_y, ny, send3, recv3, 2)
    lax.fori_loop(5, 10, pair_block, 0)

    arrived(recv3, ny - 1, 2)
    for h in range(2):
        for s in range(2):
            tiles = [recv3[h * 8 + j, s * 8 : s * 8 + 8, :] for j in range(8)]
            for c, tile in enumerate(swap_blocks(tiles, 16)):
                mid_b[h, pl.ds(s * 64 + c, 8, stride=8), :] = tile
    back_x = jnp.concatenate([mid_b[0], mid_b[1]], axis=1).T
    send4[...] = table_times(tab, back_x).reshape(32, 8, LANES)
    exchange("gx", me_x, nx, send4, recv4, 3)
    lax.fori_loop(10, 16, pair_block, 0)

    arrived(recv4, nx - 1, 3)
    halves = []
    for h in range(2):
        tiles = [recv4[h * 16 + j] for j in range(16)]
        halves.append(jnp.concatenate(swap_blocks(tiles, 8), axis=0))
    final = times_table(jnp.concatenate(halves, axis=1), tab)
    for h in range(2):
        for y in range(16):
            stress[h, pl.ds(y, 8, stride=16), :] = final[y * 8 : y * 8 + 8, h * LANES : (h + 1) * LANES]
    stores = [
        pltpu.make_async_copy(
            stress.at[h], stress_hbm.at[:, pl.ds(h * LANES, LANES)], store_sem.at[h]
        )
        for h in range(2)
    ]
    for store in stores:
        store.start()

    tall = jnp.concatenate([final[:, :LANES], final[:, LANES:]], axis=0).T
    high, low = parts(tall)
    depth = place & 127
    tau_rows = []
    for b in range(16):
        picked = hot[:, b * LANES : (b + 1) * LANES]
        lines_b = mm(high, picked) + mm(low, picked)
        at = lax.broadcasted_iota(jnp.int32, (LANES, LANES), 0)
        chosen = jnp.where(at == jnp.broadcast_to(depth[b : b + 1], (LANES, LANES)), lines_b, 0.0)
        tau_rows.append(jnp.sum(chosen, axis=0, keepdims=True))
    tau = jnp.concatenate(tau_rows, axis=0)
    pulled = pull[...].T
    burgers = [source[3 + k] for k in range(3)]
    tangent = [source[6 + k] for k in range(3)]
    for k in range(3):
        k1, k2 = (k + 1) % 3, (k + 2) % 3
        glide = burgers[k1] * tangent[k2] - burgers[k2] * tangent[k1]
        force[k] = pair_scale * pulled[k * 16 : k * 16 + 16] + tau * glide
    last = pltpu.make_async_copy(force, force_hbm, store_sem.at[2])
    last.start()
    left(send1, nx - 1, 0)
    left(send2, ny - 1, 1)
    left(send3, ny - 1, 2)
    left(send4, nx - 1, 3)
    left(pool, 8, 4)
    for store in stores:
        store.wait()
    last.wait()


def per_device(nx, ny, eigen, seg_vec, seg_off, seg_cell, blk_count, pair_list):
    f32, bf16 = jnp.float32, jnp.bfloat16
    tab = jnp.asarray(cas_table(256))
    hbm = pl.BlockSpec(memory_space=pl.ANY)
    smem = pl.BlockSpec(memory_space=pltpu.SMEM)
    vmem = pltpu.VMEM
    stress, force = pl.pallas_call(
        functools.partial(kernel, nx, ny),
        out_shape=(
            jax.ShapeDtypeStruct((128, 256), f32),
            jax.ShapeDtypeStruct((3, 16, LANES), f32),
        ),
        in_specs=[hbm, hbm, hbm, hbm, smem, smem, hbm],
        out_specs=(hbm, hbm),
        scratch_shapes=[
            vmem((2, 128, LANES), f32),
            vmem((6, 16, LANES), f32),
            vmem((3, 16, LANES), f32),
            vmem((16, LANES), jnp.int32),
            vmem((2, 256, 256), bf16),
            vmem((32, 8, LANES), f32),
            vmem((32, 8, LANES), f32),
            vmem((16, 16, LANES), f32),
            vmem((16, 16, LANES), f32),
            vmem((16, 16, LANES), f32),
            vmem((16, 16, LANES), f32),
            vmem((32, 8, LANES), f32),
            vmem((32, 8, LANES), f32),
            vmem((2, 128, LANES), f32),
            vmem((2, 128, LANES), f32),
            vmem((256, LANES), f32),
            vmem((ROWS, 16, LANES), f32),
            vmem((9, ROWS, 16, LANES), f32),
            vmem((16, 16, LANES), f32),
            vmem((ROWS, LANES, LANES), f32),
            vmem((8, ROWS, 8, LANES), f32),
            vmem((LANES, LANES), f32),
            vmem((256, 2048), bf16),
            vmem((2, 128, LANES), f32),
            vmem((3, 16, LANES), f32),
            pltpu.SemaphoreType.DMA((6,)),
            pltpu.SemaphoreType.DMA((5,)),
            pltpu.SemaphoreType.DMA((5,)),
            pltpu.SemaphoreType.DMA((3,)),
        ],
        compiler_params=pltpu.CompilerParams(
            collective_id=0, has_side_effects=True, vmem_limit_bytes=32 * 1024 * 1024
        ),
    )(
        eigen.reshape(128, 256),
        seg_vec.reshape(6, 16, LANES),
        seg_off.reshape(3, 16, LANES),
        seg_cell.reshape(16, LANES),
        blk_count.reshape(16),
        pair_list.reshape(16, 8).T,
        tab,
    )
    return stress.reshape(8, 16, 256), force.reshape(3, 1, 1, 2048)


def solution(mesh):
    return jax.shard_map(
        functools.partial(per_device, mesh.shape["gx"], mesh.shape["gy"]),
        mesh=mesh,
        in_specs=(
            P("gx", "gy", None),
            P(None, "gx", "gy", None),
            P(None, "gx", "gy", None),
            P("gx", "gy", None),
            P("gx", "gy", None),
            P("gx", "gy", None, None),
        ),
        out_specs=(P("gx", "gy", None), P(None, "gx", "gy", None)),
        check_vma=False,
    )
```

```python
import functools
import math

import jax
import jax.numpy as jnp
import ml_dtypes
import numpy as np
from jax import lax
from jax.experimental import pallas as pl
from jax.experimental.pallas import tpu as pltpu
from jax.sharding import PartitionSpec as P

nu_copper = 0.34
core_sq = 4.0
pair_scale = 4.0

MESH = pl.DeviceIdType.MESH
ROWS = 9
LANES = 128


def cas_table(length):
    steps = np.arange(length)
    angle = (steps[:, None] * steps[None, :] % length) * (2.0 * math.pi / length)
    table = np.cos(angle) + np.sin(angle)
    high = table.astype(ml_dtypes.bfloat16)
    low = (table - high.astype(np.float64)).astype(ml_dtypes.bfloat16)
    return np.stack([high, low])


def parts(x):
    high = x.astype(jnp.bfloat16)
    return high, (x - high.astype(jnp.float32)).astype(jnp.bfloat16)


def mm(a, b):
    return jnp.dot(a, b, preferred_element_type=jnp.float32)


def times_table(x, tab):
    high, low = parts(x)
    return mm(high, tab[0]) + (mm(low, tab[0]) + mm(high, tab[1]))


def table_times(tab, x):
    high, low = parts(x)
    return mm(tab[0], high) + (mm(tab[0], low) + mm(tab[1], high))


def swap_blocks(tiles, width):
    count = len(tiles)
    lane = lax.broadcasted_iota(jnp.int32, (8, LANES), 1) // width
    tiles = list(tiles)
    bit = 1
    while bit < count:
        keep = (lane & bit) == 0
        shift = bit * width
        for i in range(count):
            if i & bit:
                continue
            a, c = tiles[i], tiles[i | bit]
            tiles[i] = jnp.where(keep, a, pltpu.roll(c, shift, 1))
            tiles[i | bit] = jnp.where(keep, pltpu.roll(a, LANES - shift, 1), c)
        bit *= 2
    return tiles


def kernel(
    nx, ny, eigen_hbm, vec_hbm, off_hbm, cell_hbm, count_hbm, pair_hbm, tab_hbm,
    stress_hbm, force_hbm,
    eigen, vec, off, cell, count_ref, pair_ref, tab, send1, recv1, send2, recv2, send3, recv3, send4, recv4,
    mid_a, mid_b, gain, source, pool, by_block, own_wide, far_wide, sums, pull, hot, stress, force,
    load_sem, send_sem, recv_sem, store_sem,
):
    me_x = lax.axis_index("gx")
    me_y = lax.axis_index("gy")

    barrier = pltpu.get_barrier_semaphore()

    def greet_x(i, _):
        pl.semaphore_signal(barrier, inc=1, device_id={"gx": lax.rem(me_x + i, nx)}, device_id_type=MESH)
        return 0

    def greet_y(i, _):
        pl.semaphore_signal(barrier, inc=1, device_id={"gy": lax.rem(me_y + i, ny)}, device_id_type=MESH)
        return 0

    lax.fori_loop(1, nx, greet_x, 0)
    lax.fori_loop(1, ny, greet_y, 0)
    for dx in (-1, 1):
        for dy in (-1, 1):
            peer = {"gx": lax.rem(me_x + dx + nx, nx), "gy": lax.rem(me_y + dy + ny, ny)}
            pl.semaphore_signal(barrier, inc=1, device_id=peer, device_id_type=MESH)

    loads = [
        pltpu.make_async_copy(src, dst, load_sem.at[n])
        for n, (src, dst) in enumerate(
            (
                (eigen_hbm.at[:, pl.ds(0, LANES)], eigen.at[0]),
                (eigen_hbm.at[:, pl.ds(LANES, LANES)], eigen.at[1]),
                (tab_hbm, tab),
                (vec_hbm, vec),
                (off_hbm, off),
                (cell_hbm, cell),
                (count_hbm, count_ref),
                (pair_hbm, pair_ref),
            )
        )
    ]
    for load in loads:
        load.start()
    for load in loads[:3]:
        load.wait()

    lines = jnp.concatenate(
        [
            jnp.concatenate([eigen[h, pl.ds(y, 8, stride=16), :] for h in range(2)], axis=1)
            for y in range(16)
        ],
        axis=0,
    )
    zeta = times_table(lines, tab)
    for h in range(2):
        tiles = [zeta[y * 8 : y * 8 + 8, h * LANES : (h + 1) * LANES] for y in range(16)]
        for j, tile in enumerate(swap_blocks(tiles, 8)):
            send1[h * 16 + j] = tile

    pl.semaphore_wait(barrier, nx - 1 + ny - 1 + 4)

    def swing(k, middle):
        return middle + ((k + 1) >> 1) * (1 - 2 * (k & 1))

    def exchange(axis, me, count, send, recv, stage):
        inner = count // 8
        outer_me, inner_me = lax.div(me, inner), lax.rem(me, inner)

        def push(i, _):
            outer = lax.rem(outer_me + swing(lax.div(i, inner), 4), 8)
            peer = outer * inner + lax.rem(inner_me + swing(lax.rem(i, inner), inner // 2), inner)
            pltpu.make_async_remote_copy(
                src_ref=send.at[peer], dst_ref=recv.at[me], send_sem=send_sem.at[stage],
                recv_sem=recv_sem.at[stage], device_id={axis: peer}, device_id_type=MESH,
            ).start()
            return 0

        lax.fori_loop(0, count - 1, push, 0)
        recv[me] = send[me]

    def arrived(buffer, count, stage):
        whole = buffer.at[pl.ds(0, count)]
        pltpu.make_async_copy(whole, whole, recv_sem.at[stage]).wait()

    def left(buffer, count, stage):
        whole = buffer.at[pl.ds(0, count)]
        pltpu.make_async_copy(whole, whole, send_sem.at[stage]).wait()

    exchange("gx", me_x, nx, send1, recv1, 0)

    for load in loads[3:]:
        load.wait()
    row_id = lax.broadcasted_iota(jnp.int32, (16, LANES), 0)
    lane_id = lax.broadcasted_iota(jnp.int32, (16, LANES), 1)
    counts = jnp.zeros((16, LANES), jnp.int32)
    for b in range(16):
        counts = jnp.where(row_id == b, count_ref[0, b], counts)
    live = jnp.where(lane_id < counts, 1.0, 0.0)
    place = cell[...]
    spots = (place >> 12, (place >> 8) & 15, place & 255)
    for k in range(3):
        source[k] = spots[k].astype(jnp.float32) + off[k]
        source[3 + k] = vec[k] * live
        source[6 + k] = vec[3 + k]
    for dx in (-1, 0, 1):
        for dy in (-1, 0, 1):
            if dx == 0 and dy == 0:
                continue
            peer = {"gx": lax.rem(me_x + dx + nx, nx), "gy": lax.rem(me_y + dy + ny, ny)}
            pltpu.make_async_remote_copy(
                src_ref=source, dst_ref=pool.at[(1 - dx) * 3 + (1 - dy)], send_sem=send_sem.at[4],
                recv_sem=recv_sem.at[4], device_id=peer, device_id_type=MESH,
            ).start()
    for r in range(ROWS):
        pool[4, r] = source[r]

    for r in range(ROWS):
        rows = source[r]
        for b in range(16):
            by_block[b, pl.ds(r, 1), :] = rows[b : b + 1]

    def widen(b, _):
        columns = by_block[b].T
        for r in range(ROWS):
            own_wide[b, r] = jnp.broadcast_to(columns[:, r : r + 1], (LANES, LANES))
        return 0

    lax.fori_loop(0, 16, widen, 0)

    def wave(index):
        sine = 2.0 * jnp.sin(index.astype(jnp.float32) * (math.pi / 256.0))
        return sine * sine

    lane_row = lax.broadcasted_iota(jnp.int32, (8, LANES), 1)
    freq_z = me_x * 8 + (lane_row >> 4)
    freq_x = me_y * 16 + (lane_row & 15)
    wave_x, wave_z = wave(freq_x), wave(freq_z)
    both = wave_x + wave_z
    product = 2.0 / (1.0 - nu_copper) * wave_x * wave_z
    corner = (freq_x == 0) & (freq_z == 0)

    def fill_gain(i, _):
        freq_y = i * 8 + lax.broadcasted_iota(jnp.int32, (8, LANES), 0)
        total = both + wave(freq_y)
        safe = jnp.where(corner & (freq_y == 0), 1.0, total)
        inverse = 1.0 / safe
        gain[pl.ds(pl.multiple_of(i * 8, 8), 8), :] = (-2.0 / 256.0**3) * (
            1.0 - both * inverse + product * inverse * inverse
        )
        return 0

    lax.fori_loop(0, 32, fill_gain, 0)

    spot = ((place >> 7) & 1) * 128 + ((place >> 8) & 15) * 8 + (place >> 12)
    for b in range(16):
        want = jnp.broadcast_to(spot[b : b + 1], (256, LANES))
        at = lax.broadcasted_iota(jnp.int32, (256, LANES), 0)
        hot[:, b * LANES : (b + 1) * LANES] = jnp.where(want == at, 1.0, 0.0).astype(jnp.bfloat16)

    arrived(recv1, nx - 1, 0)
    held = recv1[...].reshape(256, LANES)
    along_x = times_table(held.T, tab)
    for h in range(2):
        mid_a[h] = along_x[:, h * LANES : (h + 1) * LANES]
    for h in range(2):
        for s in range(2):
            tiles = [mid_a[h, pl.ds(s * 64 + c, 8, stride=8), :] for c in range(8)]
            for j, tile in enumerate(swap_blocks(tiles, 16)):
                send2[h * 8 + j, s * 8 : s * 8 + 8, :] = tile
    exchange("gy", me_y, ny, send2, recv2, 1)

    arrived(pool, 8, 4)
    for p in range(3):
        for q in range(3):
            if p != 1:
                pool[p * 3 + q, 0] += (p - 1) * 8.0
            if q != 1:
                pool[p * 3 + q, 1] += (q - 1) * 16.0

    def pair_block(b, _):
        for n in range(8):
            partner = pair_ref[n, b]
            device = partner >> 4
            slot = partner & 15
            for r in range(ROWS):
                far_wide[n, r] = jnp.broadcast_to(pool[device, r, pl.ds(slot, 1), :], (8, LANES))

        def tile(i, _):
            rows = pl.ds(pl.multiple_of(i * 8, 8), 8)
            own = [own_wide[b, r, rows, :] for r in range(ROWS)]
            triple = [3.0 * own[3 + k] for k in range(3)]
            total = [jnp.zeros((8, LANES), jnp.float32) for _ in range(3)]
            for n in range(8):
                far = [far_wide[n, r] for r in range(ROWS)]
                delta = [own[k] - far[k] for k in range(3)]
                square = (delta[0] * delta[0] + core_sq) + (delta[1] * delta[1] + delta[2] * delta[2])
                inverse = lax.rsqrt(square)
                inv_two = inverse * inverse
                inv_three = inv_two * inverse
                burg_dot = own[3] * far[3] + own[4] * far[4] + own[5] * far[5]
                line_dot = own[6] * far[6] + own[7] * far[7] + own[8] * far[8]
                burg_own = triple[0] * delta[0] + triple[1] * delta[1] + triple[2] * delta[2]
                burg_far = far[3] * delta[0] + far[4] * delta[1] + far[5] * delta[2]
                weight = (line_dot * inv_three) * (burg_dot - (burg_own * burg_far) * inv_two)
                total = [total[k] + weight * delta[k] for k in range(3)]
            for k in range(3):
                sums[k, rows, :] = total[k]
            return 0

        lax.fori_loop(0, 16, tile, 0)
        lane = lax.broadcasted_iota(jnp.int32, (LANES, LANES), 1)
        have = pull[...]
        for k in range(3):
            have = jnp.where(lane == k * 16 + b, jnp.sum(sums[k], axis=1, keepdims=True), have)
        pull[...] = have
        return 0

    pull[...] = jnp.zeros_like(pull)
    lax.fori_loop(0, 5, pair_block, 0)

    arrived(recv2, ny - 1, 1)
    spectrum = table_times(tab, recv2[...].reshape(256, LANES)) * gain[...]
    send3[...] = table_times(tab, spectrum).reshape(16, 16, LANES)
    exchange("gy", me_y, ny, send3, recv3, 2)
    lax.fori_loop(5, 10, pair_block, 0)

    arrived(recv3, ny - 1, 2)
    for h in range(2):
        for s in range(2):
            tiles = [recv3[h * 8 + j, s * 8 : s * 8 + 8, :] for j in range(8)]
            for c, tile in enumerate(swap_blocks(tiles, 16)):
                mid_b[h, pl.ds(s * 64 + c, 8, stride=8), :] = tile
    back_x = jnp.concatenate([mid_b[0], mid_b[1]], axis=1).T
    send4[...] = table_times(tab, back_x).reshape(32, 8, LANES)
    exchange("gx", me_x, nx, send4, recv4, 3)
    lax.fori_loop(10, 16, pair_block, 0)

    arrived(recv4, nx - 1, 3)
    halves = []
    for h in range(2):
        tiles = [recv4[h * 16 + j] for j in range(16)]
        halves.append(jnp.concatenate(swap_blocks(tiles, 8), axis=0))
    final = times_table(jnp.concatenate(halves, axis=1), tab)
    for h in range(2):
        for y in range(16):
            stress[h, pl.ds(y, 8, stride=16), :] = final[y * 8 : y * 8 + 8, h * LANES : (h + 1) * LANES]
    stores = [
        pltpu.make_async_copy(
            stress.at[h], stress_hbm.at[:, pl.ds(h * LANES, LANES)], store_sem.at[h]
        )
        for h in range(2)
    ]
    for store in stores:
        store.start()

    tall = jnp.concatenate([final[:, :LANES], final[:, LANES:]], axis=0).T
    high, low = parts(tall)
    depth = place & 127
    tau_rows = []
    for b in range(16):
        picked = hot[:, b * LANES : (b + 1) * LANES]
        lines_b = mm(high, picked) + mm(low, picked)
        at = lax.broadcasted_iota(jnp.int32, (LANES, LANES), 0)
        chosen = jnp.where(at == jnp.broadcast_to(depth[b : b + 1], (LANES, LANES)), lines_b, 0.0)
        tau_rows.append(jnp.sum(chosen, axis=0, keepdims=True))
    tau = jnp.concatenate(tau_rows, axis=0)
    pulled = pull[...].T
    burgers = [source[3 + k] for k in range(3)]
    tangent = [source[6 + k] for k in range(3)]
    for k in range(3):
        k1, k2 = (k + 1) % 3, (k + 2) % 3
        glide = burgers[k1] * tangent[k2] - burgers[k2] * tangent[k1]
        force[k] = pair_scale * pulled[k * 16 : k * 16 + 16] + tau * glide
    last = pltpu.make_async_copy(force, force_hbm, store_sem.at[2])
    last.start()
    left(send1, nx - 1, 0)
    left(send2, ny - 1, 1)
    left(send3, ny - 1, 2)
    left(send4, nx - 1, 3)
    left(pool, 8, 4)
    for store in stores:
        store.wait()
    last.wait()


def per_device(nx, ny, eigen, seg_vec, seg_off, seg_cell, blk_count, pair_list):
    f32, bf16 = jnp.float32, jnp.bfloat16
    tab = jnp.asarray(cas_table(256))
    hbm = pl.BlockSpec(memory_space=pl.ANY)
    vmem = pltpu.VMEM
    stress, force = pl.pallas_call(
        functools.partial(kernel, nx, ny),
        out_shape=(
            jax.ShapeDtypeStruct((128, 256), f32),
            jax.ShapeDtypeStruct((3, 16, LANES), f32),
        ),
        in_specs=[hbm] * 7,
        out_specs=(hbm, hbm),
        scratch_shapes=[
            vmem((2, 128, LANES), f32),
            vmem((6, 16, LANES), f32),
            vmem((3, 16, LANES), f32),
            vmem((16, LANES), jnp.int32),
            pltpu.SMEM((1, 16), jnp.int32),
            pltpu.SMEM((8, 16), jnp.int32),
            vmem((2, 256, 256), bf16),
            vmem((32, 8, LANES), f32),
            vmem((32, 8, LANES), f32),
            vmem((16, 16, LANES), f32),
            vmem((16, 16, LANES), f32),
            vmem((16, 16, LANES), f32),
            vmem((16, 16, LANES), f32),
            vmem((32, 8, LANES), f32),
            vmem((32, 8, LANES), f32),
            vmem((2, 128, LANES), f32),
            vmem((2, 128, LANES), f32),
            vmem((256, LANES), f32),
            vmem((ROWS, 16, LANES), f32),
            vmem((9, ROWS, 16, LANES), f32),
            vmem((16, 16, LANES), f32),
            vmem((16, ROWS, LANES, LANES), f32),
            vmem((8, ROWS, 8, LANES), f32),
            vmem((3, LANES, LANES), f32),
            vmem((LANES, LANES), f32),
            vmem((256, 2048), bf16),
            vmem((2, 128, LANES), f32),
            vmem((3, 16, LANES), f32),
            pltpu.SemaphoreType.DMA((8,)),
            pltpu.SemaphoreType.DMA((5,)),
            pltpu.SemaphoreType.DMA((5,)),
            pltpu.SemaphoreType.DMA((3,)),
        ],
        compiler_params=pltpu.CompilerParams(
            collective_id=0, has_side_effects=True, vmem_limit_bytes=60 * 1024 * 1024
        ),
    )(
        eigen.reshape(128, 256),
        seg_vec.reshape(6, 16, LANES),
        seg_off.reshape(3, 16, LANES),
        seg_cell.reshape(16, LANES),
        blk_count.reshape(1, 16),
        pair_list.reshape(16, 8).T,
        tab,
    )
    return stress.reshape(8, 16, 256), force.reshape(3, 1, 1, 2048)


def solution(mesh):
    return jax.shard_map(
        functools.partial(per_device, mesh.shape["gx"], mesh.shape["gy"]),
        mesh=mesh,
        in_specs=(
            P("gx", "gy", None),
            P(None, "gx", "gy", None),
            P(None, "gx", "gy", None),
            P("gx", "gy", None),
            P("gx", "gy", None),
            P("gx", "gy", None, None),
        ),
        out_specs=(P("gx", "gy", None), P(None, "gx", "gy", None)),
        check_vma=False,
    )
```

```python
import functools
import math

import jax
import jax.numpy as jnp
import ml_dtypes
import numpy as np
from jax import lax
from jax.experimental import pallas as pl
from jax.experimental.pallas import tpu as pltpu
from jax.sharding import PartitionSpec as P

nu_copper = 0.34
core_sq = 4.0
pair_scale = 4.0

MESH = pl.DeviceIdType.MESH
ROWS = 9
LANES = 128
CUT = (5, 10)


def cas_table(length):
    steps = np.arange(length)
    angle = (steps[:, None] * steps[None, :] % length) * (2.0 * math.pi / length)
    table = np.cos(angle) + np.sin(angle)
    high = table.astype(ml_dtypes.bfloat16)
    low = (table - high.astype(np.float64)).astype(ml_dtypes.bfloat16)
    return np.stack([high, low])


def parts(x):
    high = x.astype(jnp.bfloat16)
    return high, (x - high.astype(jnp.float32)).astype(jnp.bfloat16)


def three_parts(x):
    high = x.astype(jnp.bfloat16)
    rest = x - high.astype(jnp.float32)
    return high, *parts(rest)


def mm(a, b):
    return jnp.dot(a, b, preferred_element_type=jnp.float32)


def times_table(x, tab):
    high, low = parts(x)
    return mm(high, tab[0]) + (mm(low, tab[0]) + mm(high, tab[1]))


def table_times(tab, x):
    high, low = parts(x)
    return mm(tab[0], high) + (mm(tab[0], low) + mm(tab[1], high))


def swap_blocks(tiles, width):
    count = len(tiles)
    lane = lax.broadcasted_iota(jnp.int32, (8, LANES), 1) // width
    tiles = list(tiles)
    bit = 1
    while bit < count:
        keep = (lane & bit) == 0
        shift = bit * width
        for i in range(count):
            if i & bit:
                continue
            a, c = tiles[i], tiles[i | bit]
            tiles[i] = jnp.where(keep, a, pltpu.roll(c, shift, 1))
            tiles[i | bit] = jnp.where(keep, pltpu.roll(a, LANES - shift, 1), c)
        bit *= 2
    return tiles


def kernel(
    nx, ny, eigen_hbm, vec_hbm, off_hbm, cell_hbm, count_hbm, pair_hbm, tab_hbm, wave_hbm,
    stress, force,
    eigen, vec, off, cell, count_ref, pair_ref, tab, wave, send1, recv1, send2, recv2, send3, recv3, send4, recv4,
    mid_a, mid_b, gain, source, pool, by_block, own_wide, far_wide, sums, pull, hot,
    load_sem, send_sem, recv_sem,
):
    me_x = lax.axis_index("gx")
    me_y = lax.axis_index("gy")

    def swing(k, middle):
        return middle + ((k + 1) >> 1) * (1 - 2 * (k & 1))

    def peer_of(me, count, i):
        inner = count // 8
        outer = ((me // inner) + swing(i // inner, 4)) & 7
        return outer * inner + ((me + swing(i % inner, inner // 2)) & (inner - 1))

    loads = [
        pltpu.make_async_copy(src, dst, load_sem.at[n])
        for n, (src, dst) in enumerate(
            (
                (eigen_hbm.at[:, pl.ds(0, LANES)], eigen.at[0]),
                (eigen_hbm.at[:, pl.ds(LANES, LANES)], eigen.at[1]),
                (tab_hbm, tab),
                (vec_hbm, vec),
                (off_hbm, off),
                (cell_hbm, cell),
                (count_hbm, count_ref),
                (pair_hbm, pair_ref),
                (wave_hbm, wave),
            )
        )
    ]
    for load in loads:
        load.start()

    barrier = pltpu.get_barrier_semaphore()

    for axis, me, count in (("gx", me_x, nx), ("gy", me_y, ny)):
        for i in range(count - 1):
            pl.semaphore_signal(
                barrier, inc=1, device_id={axis: peer_of(me, count, i)}, device_id_type=MESH
            )

    for load in loads[:3]:
        load.wait()

    lines = jnp.concatenate(
        [
            jnp.concatenate([eigen[h, pl.ds(y, 8, stride=16), :] for h in range(2)], axis=1)
            for y in range(16)
        ],
        axis=0,
    )
    zeta = times_table(lines, tab)
    for h in range(2):
        tiles = [zeta[y * 8 : y * 8 + 8, h * LANES : (h + 1) * LANES] for y in range(16)]
        for j, tile in enumerate(swap_blocks(tiles, 8)):
            send1[h * 16 + j] = tile

    pl.semaphore_wait(barrier, nx - 1 + ny - 1)

    def exchange(axis, me, count, send, recv, stage):
        for i in range(count - 1):
            peer = peer_of(me, count, i)
            pltpu.make_async_remote_copy(
                src_ref=send.at[peer], dst_ref=recv.at[me], send_sem=send_sem.at[stage],
                recv_sem=recv_sem.at[stage], device_id={axis: peer}, device_id_type=MESH,
            ).start()
        recv[me] = send[me]

    def arrived(buffer, count, stage):
        whole = buffer.at[pl.ds(0, count)]
        pltpu.make_async_copy(whole, whole, recv_sem.at[stage]).wait()

    def left(buffer, count, stage):
        whole = buffer.at[pl.ds(0, count)]
        pltpu.make_async_copy(whole, whole, send_sem.at[stage]).wait()

    exchange("gx", me_x, nx, send1, recv1, 0)

    for load in loads[3:]:
        load.wait()
    row_id = lax.broadcasted_iota(jnp.int32, (16, LANES), 0)
    lane_id = lax.broadcasted_iota(jnp.int32, (16, LANES), 1)
    counts = jnp.zeros((16, LANES), jnp.int32)
    for b in range(16):
        counts = jnp.where(row_id == b, count_ref[0, b], counts)
    live = jnp.where(lane_id < counts, 1.0, 0.0)
    place = cell[...]
    spots = (place >> 12, (place >> 8) & 15, place & 255)
    for k in range(3):
        source[k] = spots[k].astype(jnp.float32) + off[k]
        source[3 + k] = vec[k] * live
        source[6 + k] = vec[3 + k]

    def pass_on(column, p, q, axis, me, count, step, stage):
        pltpu.make_async_remote_copy(
            src_ref=column, dst_ref=pool.at[p * 3 + q], send_sem=send_sem.at[4], recv_sem=recv_sem.at[stage],
            device_id={axis: (me + step) & (count - 1)}, device_id_type=MESH,
        ).start()

    for step in (-1, 1):
        pass_on(source, 1 - step, 1, "gx", me_x, nx, step, 4)
    for step in (-1, 1):
        pass_on(source, 1, 1 - step, "gy", me_y, ny, step, 5)
    for r in range(ROWS):
        pool[4, r] = source[r]

    by_block[...] = jnp.zeros_like(by_block)
    for r in range(ROWS):
        rows = source[r]
        for b in range(16):
            by_block[b, pl.ds(r, 1), :] = rows[b : b + 1]

    row = lax.broadcasted_iota(jnp.int32, (48, ROWS * LANES), 0) & 15
    spread = jnp.where(row == lax.broadcasted_iota(jnp.int32, (48, ROWS * LANES), 1) >> 7, 1.0, 0.0)
    spread = spread.astype(jnp.bfloat16)

    def widen(b, _):
        rows = jnp.concatenate([part.astype(jnp.float32) for part in three_parts(by_block[b])], axis=0)
        wide = mm(rows.T.astype(jnp.bfloat16), spread)
        for r in range(ROWS):
            own_wide[b, r] = wide[:, r * LANES : (r + 1) * LANES]
        return 0

    lax.fori_loop(0, 16, widen, 0, unroll=4)

    arrived(pool, 2, 4)
    for step in (-1, 1):
        for p in (0, 2):
            pass_on(pool.at[p * 3 + 1], p, 1 - step, "gy", me_y, ny, step, 5)

    lane = lax.broadcasted_iota(jnp.int32, (8, LANES), 1)
    freq_z = me_x * 8 + (lane >> 4)
    freq_x = me_y * 16 + (lane & 15)

    def wave_of(index):
        sine = 2.0 * jnp.sin(index.astype(jnp.float32) * (math.pi / 256.0))
        return sine * sine

    wave_x, wave_z = wave_of(freq_x), wave_of(freq_z)
    both = wave_x + wave_z
    product = 2.0 / (1.0 - nu_copper) * wave_x * wave_z
    corner = (freq_x == 0) & (freq_z == 0)
    for i in range(32):
        total = both + wave[pl.ds(i * 8, 8), :]
        if i == 0:
            total = jnp.where(corner & (lax.broadcasted_iota(jnp.int32, (8, LANES), 0) == 0), 1.0, total)
        inverse = 1.0 / total
        gain[pl.ds(i * 8, 8), :] = (-2.0 / 256.0**3) * (1.0 - both * inverse + product * inverse * inverse)

    spot = ((place >> 7) & 1) * 128 + ((place >> 8) & 15) * 8 + (place >> 12)
    for b in range(16):
        want = jnp.broadcast_to(spot[b : b + 1], (256, LANES))
        at = lax.broadcasted_iota(jnp.int32, (256, LANES), 0)
        hot[:, b * LANES : (b + 1) * LANES] = jnp.where(want == at, 1.0, 0.0).astype(jnp.bfloat16)

    def pair_block(b, _):
        for n in range(8):
            partner = pair_ref[n, b]
            device = partner >> 4
            slot = partner & 15
            shift = {0: (lax.div(device, 3) - 1) * 8, 1: (lax.rem(device, 3) - 1) * 16}
            for r in range(ROWS):
                far = pool[device, r, pl.ds(slot, 1), :]
                if r in shift:
                    far = far + shift[r].astype(jnp.float32)
                far_wide[n, r] = jnp.broadcast_to(far, (8, LANES))

        def tile(i, _):
            rows = pl.ds(pl.multiple_of(i * 8, 8), 8)
            own = [own_wide[b, r, rows, :] for r in range(ROWS)]
            triple = [3.0 * own[3 + k] for k in range(3)]
            total = [jnp.zeros((8, LANES), jnp.float32) for _ in range(3)]
            for n in range(8):
                far = [far_wide[n, r] for r in range(ROWS)]
                delta = [own[k] - far[k] for k in range(3)]
                square = (delta[0] * delta[0] + core_sq) + (delta[1] * delta[1] + delta[2] * delta[2])
                inverse = lax.rsqrt(square)
                inv_two = inverse * inverse
                inv_three = inv_two * inverse
                burg_dot = own[3] * far[3] + own[4] * far[4] + own[5] * far[5]
                line_dot = own[6] * far[6] + own[7] * far[7] + own[8] * far[8]
                burg_own = triple[0] * delta[0] + triple[1] * delta[1] + triple[2] * delta[2]
                burg_far = far[3] * delta[0] + far[4] * delta[1] + far[5] * delta[2]
                weight = (line_dot * inv_three) * (burg_dot - (burg_own * burg_far) * inv_two)
                total = [total[k] + weight * delta[k] for k in range(3)]
            for k in range(3):
                sums[b, k, rows, :] = total[k]
            return 0

        lax.fori_loop(0, 16, tile, 0)
        return 0

    def pair_blocks(first, end):
        lax.fori_loop(first, end, pair_block, 0)
        column = lax.broadcasted_iota(jnp.int32, (2 * LANES, LANES), 1)
        have = pull[...]
        for b in range(first, end):
            for k in range(3):
                pick = jnp.where(column == k * 16 + b, 1.0, 0.0).astype(jnp.bfloat16)
                have = have + mm(jnp.concatenate(parts(sums[b, k]), axis=1), pick)
        pull[...] = have

    pull[...] = jnp.zeros_like(pull)

    arrived(recv1, nx - 1, 0)
    held = recv1[...].reshape(256, LANES)
    along_x = times_table(held.T, tab)
    for h in range(2):
        mid_a[h] = along_x[:, h * LANES : (h + 1) * LANES]
    for h in range(2):
        for s in range(2):
            tiles = [mid_a[h, pl.ds(s * 64 + c, 8, stride=8), :] for c in range(8)]
            for j, tile in enumerate(swap_blocks(tiles, 16)):
                send2[h * 8 + j, s * 8 : s * 8 + 8, :] = tile
    exchange("gy", me_y, ny, send2, recv2, 1)

    arrived(pool, 6, 5)
    pair_blocks(0, CUT[0])

    arrived(recv2, ny - 1, 1)
    spectrum = table_times(tab, recv2[...].reshape(256, LANES)) * gain[...]
    send3[...] = table_times(tab, spectrum).reshape(16, 16, LANES)
    exchange("gy", me_y, ny, send3, recv3, 2)
    pair_blocks(CUT[0], CUT[1])

    arrived(recv3, ny - 1, 2)
    for h in range(2):
        for s in range(2):
            tiles = [recv3[h * 8 + j, s * 8 : s * 8 + 8, :] for j in range(8)]
            for c, tile in enumerate(swap_blocks(tiles, 16)):
                mid_b[h, pl.ds(s * 64 + c, 8, stride=8), :] = tile
    back_x = jnp.concatenate([mid_b[0], mid_b[1]], axis=1).T
    send4[...] = table_times(tab, back_x).reshape(32, 8, LANES)
    exchange("gx", me_x, nx, send4, recv4, 3)
    pair_blocks(CUT[1], 16)

    arrived(recv4, nx - 1, 3)
    halves = []
    for h in range(2):
        tiles = [recv4[h * 16 + j] for j in range(16)]
        halves.append(jnp.concatenate(swap_blocks(tiles, 8), axis=0))
    final = times_table(jnp.concatenate(halves, axis=1), tab)
    for h in range(2):
        for y in range(16):
            stress[pl.ds(h * 128 + y, 8, stride=16), :] = final[y * 8 : y * 8 + 8, h * LANES : (h + 1) * LANES]
    tall = jnp.concatenate([final[:, :LANES], final[:, LANES:]], axis=0).T
    high, low = parts(tall)
    depth = place & 127
    tau_rows = []
    for b in range(16):
        picked = hot[:, b * LANES : (b + 1) * LANES]
        lines_b = mm(high, picked) + mm(low, picked)
        at = lax.broadcasted_iota(jnp.int32, (LANES, LANES), 0)
        chosen = jnp.where(at == jnp.broadcast_to(depth[b : b + 1], (LANES, LANES)), lines_b, 0.0)
        tau_rows.append(jnp.sum(chosen, axis=0, keepdims=True))
    tau = jnp.concatenate(tau_rows, axis=0)
    pulled = pull[...].T
    burgers = [source[3 + k] for k in range(3)]
    tangent = [source[6 + k] for k in range(3)]
    for k in range(3):
        k1, k2 = (k + 1) % 3, (k + 2) % 3
        glide = burgers[k1] * tangent[k2] - burgers[k2] * tangent[k1]
        force[k] = pair_scale * pulled[k * 16 : k * 16 + 16] + tau * glide
    left(send1, nx - 1, 0)
    left(send2, ny - 1, 1)
    left(send3, ny - 1, 2)
    left(send4, nx - 1, 3)
    left(pool, 8, 4)


def per_device(nx, ny, eigen, seg_vec, seg_off, seg_cell, blk_count, pair_list):
    f32, bf16 = jnp.float32, jnp.bfloat16
    tab = jnp.asarray(cas_table(256))
    sines = 2.0 * np.sin(np.arange(256) * (math.pi / 256.0))
    wave = jnp.asarray(np.repeat((sines * sines).astype(np.float32)[:, None], LANES, axis=1))
    hbm = pl.BlockSpec(memory_space=pltpu.HBM)
    out = pl.BlockSpec(memory_space=pltpu.VMEM)
    vmem = pltpu.VMEM
    stress, force = pl.pallas_call(
        functools.partial(kernel, nx, ny),
        out_shape=(
            vmem((256, LANES), f32),
            vmem((3, 16, LANES), f32),
        ),
        in_specs=[hbm] * 8,
        out_specs=(out, out),
        scratch_shapes=[
            vmem((2, 128, LANES), f32),
            vmem((6, 16, LANES), f32),
            vmem((3, 16, LANES), f32),
            vmem((16, LANES), jnp.int32),
            pltpu.SMEM((1, 16), jnp.int32),
            pltpu.SMEM((8, 16), jnp.int32),
            vmem((2, 256, 256), bf16),
            vmem((256, LANES), f32),
            vmem((32, 8, LANES), f32),
            vmem((32, 8, LANES), f32),
            vmem((16, 16, LANES), f32),
            vmem((16, 16, LANES), f32),
            vmem((16, 16, LANES), f32),
            vmem((16, 16, LANES), f32),
            vmem((32, 8, LANES), f32),
            vmem((32, 8, LANES), f32),
            vmem((2, 128, LANES), f32),
            vmem((2, 128, LANES), f32),
            vmem((256, LANES), f32),
            vmem((ROWS, 16, LANES), f32),
            vmem((9, ROWS, 16, LANES), f32),
            vmem((16, 16, LANES), f32),
            vmem((16, ROWS, LANES, LANES), f32),
            vmem((8, ROWS, 8, LANES), f32),
            vmem((16, 3, LANES, LANES), f32),
            vmem((LANES, LANES), f32),
            vmem((256, 2048), bf16),
            pltpu.SemaphoreType.DMA((9,)),
            pltpu.SemaphoreType.DMA((5,)),
            pltpu.SemaphoreType.DMA((6,)),
        ],
        compiler_params=pltpu.CompilerParams(
            collective_id=0, has_side_effects=True, vmem_limit_bytes=60 * 1024 * 1024
        ),
    )(
        eigen.reshape(128, 256),
        seg_vec.reshape(6, 16, LANES),
        seg_off.reshape(3, 16, LANES),
        seg_cell.reshape(16, LANES),
        blk_count.reshape(1, 16),
        pair_list.reshape(16, 8).T,
        tab,
        wave,
    )
    stress = jnp.concatenate([stress[:128], stress[128:]], axis=1)
    return stress.reshape(8, 16, 256), force.reshape(3, 1, 1, 2048)


def solution(mesh):
    return jax.shard_map(
        functools.partial(per_device, mesh.shape["gx"], mesh.shape["gy"]),
        mesh=mesh,
        in_specs=(
            P("gx", "gy", None),
            P(None, "gx", "gy", None),
            P(None, "gx", "gy", None),
            P("gx", "gy", None),
            P("gx", "gy", None),
            P("gx", "gy", None, None),
        ),
        out_specs=(P("gx", "gy", None), P(None, "gx", "gy", None)),
        check_vma=False,
    )
```

```python
import functools
import math

import jax
import jax.numpy as jnp
import ml_dtypes
import numpy as np
from jax import lax
from jax.experimental import pallas as pl
from jax.experimental.pallas import tpu as pltpu
from jax.sharding import PartitionSpec as P

nu_copper = 0.34
core_sq = 4.0
pair_scale = 4.0

MESH = pl.DeviceIdType.MESH
ROWS = 9
LANES = 128
CUT = (5, 10)


def cas_table(length):
    steps = np.arange(length)
    angle = (steps[:, None] * steps[None, :] % length) * (2.0 * math.pi / length)
    table = np.cos(angle) + np.sin(angle)
    high = table.astype(ml_dtypes.bfloat16)
    low = (table - high.astype(np.float64)).astype(ml_dtypes.bfloat16)
    return np.stack([high, low])


def parts(x):
    high = x.astype(jnp.bfloat16)
    return high, (x - high.astype(jnp.float32)).astype(jnp.bfloat16)


def three_parts(x):
    high = x.astype(jnp.bfloat16)
    rest = x - high.astype(jnp.float32)
    return high, *parts(rest)


def mm(a, b):
    return jnp.dot(a, b, preferred_element_type=jnp.float32)


def times_table(x, tab):
    high, low = parts(x)
    return mm(high, tab[0]) + (mm(low, tab[0]) + mm(high, tab[1]))


def table_times(tab, x):
    high, low = parts(x)
    return mm(tab[0], high) + (mm(tab[0], low) + mm(tab[1], high))


def swap_blocks(tiles, width):
    count = len(tiles)
    lane = lax.broadcasted_iota(jnp.int32, (8, LANES), 1) // width
    tiles = list(tiles)
    bit = 1
    while bit < count:
        keep = (lane & bit) == 0
        shift = bit * width
        for i in range(count):
            if i & bit:
                continue
            a, c = tiles[i], tiles[i | bit]
            tiles[i] = jnp.where(keep, a, pltpu.roll(c, shift, 1))
            tiles[i | bit] = jnp.where(keep, pltpu.roll(a, LANES - shift, 1), c)
        bit *= 2
    return tiles


def kernel(
    nx, ny, eigen_hbm, vec_hbm, off_hbm, cell_hbm, count_hbm, pair_hbm, tab_hbm, wave_hbm,
    stress, force,
    eigen, vec, off, cell, count_ref, pair_ref, tab, wave, send1, recv1, send2, recv2, send3, recv3, send4, recv4,
    mid_a, mid_b, gain, source, pool, by_block, own_wide, far_wide, sums, pull, hot,
    load_sem, send_sem, recv_sem,
):
    me_x = lax.axis_index("gx")
    me_y = lax.axis_index("gy")

    def swing(k, middle):
        return middle + ((k + 1) >> 1) * (1 - 2 * (k & 1))

    def peer_of(me, count, i):
        inner = count // 8
        outer = ((me // inner) + swing(i // inner, 4)) & 7
        return outer * inner + ((me + swing(i % inner, inner // 2)) & (inner - 1))

    loads = [
        pltpu.make_async_copy(src, dst, load_sem.at[n])
        for n, (src, dst) in enumerate(
            (
                (eigen_hbm.at[:, pl.ds(0, LANES)], eigen.at[0]),
                (eigen_hbm.at[:, pl.ds(LANES, LANES)], eigen.at[1]),
                (tab_hbm, tab),
                (vec_hbm, vec),
                (off_hbm, off),
                (cell_hbm, cell),
                (count_hbm, count_ref),
                (pair_hbm, pair_ref),
                (wave_hbm, wave),
            )
        )
    ]
    for load in loads:
        load.start()

    barrier = pltpu.get_barrier_semaphore()

    for axis, me, count in (("gx", me_x, nx), ("gy", me_y, ny)):
        for i in range(count - 1):
            pl.semaphore_signal(
                barrier, inc=1, device_id={axis: peer_of(me, count, i)}, device_id_type=MESH
            )

    for load in loads[3:]:
        load.wait()
    row_id = lax.broadcasted_iota(jnp.int32, (16, LANES), 0)
    lane_id = lax.broadcasted_iota(jnp.int32, (16, LANES), 1)
    counts = jnp.zeros((16, LANES), jnp.int32)
    for b in range(16):
        counts = jnp.where(row_id == b, count_ref[0, b], counts)
    live = jnp.where(lane_id < counts, 1.0, 0.0)
    place = cell[...]
    spots = (place >> 12, (place >> 8) & 15, place & 255)
    for k in range(3):
        source[k] = spots[k].astype(jnp.float32) + off[k]
        source[3 + k] = vec[k] * live
        source[6 + k] = vec[3 + k]
    for load in loads[:3]:
        load.wait()

    lines = jnp.concatenate(
        [
            jnp.concatenate([eigen[h, pl.ds(y, 8, stride=16), :] for h in range(2)], axis=1)
            for y in range(16)
        ],
        axis=0,
    )
    zeta = times_table(lines, tab)
    for h in range(2):
        tiles = [zeta[y * 8 : y * 8 + 8, h * LANES : (h + 1) * LANES] for y in range(16)]
        for j, tile in enumerate(swap_blocks(tiles, 8)):
            send1[h * 16 + j] = tile

    pl.semaphore_wait(barrier, nx - 1 + ny - 1)

    def exchange(axis, me, count, send, recv, stage):
        for i in range(count - 1):
            peer = peer_of(me, count, i)
            pltpu.make_async_remote_copy(
                src_ref=send.at[peer], dst_ref=recv.at[me], send_sem=send_sem.at[stage],
                recv_sem=recv_sem.at[stage], device_id={axis: peer}, device_id_type=MESH,
            ).start()
        recv[me] = send[me]

    def arrived(buffer, count, stage):
        whole = buffer.at[pl.ds(0, count)]
        pltpu.make_async_copy(whole, whole, recv_sem.at[stage]).wait()

    def left(buffer, count, stage):
        whole = buffer.at[pl.ds(0, count)]
        pltpu.make_async_copy(whole, whole, send_sem.at[stage]).wait()

    def pass_on(column, p, q, axis, me, count, step, stage):
        pltpu.make_async_remote_copy(
            src_ref=column, dst_ref=pool.at[p * 3 + q], send_sem=send_sem.at[4], recv_sem=recv_sem.at[stage],
            device_id={axis: (me + step) & (count - 1)}, device_id_type=MESH,
        ).start()

    for step in (-1, 1):
        pass_on(source, 1 - step, 1, "gx", me_x, nx, step, 4)
    for step in (-1, 1):
        pass_on(source, 1, 1 - step, "gy", me_y, ny, step, 5)
    exchange("gx", me_x, nx, send1, recv1, 0)

    for r in range(ROWS):
        pool[4, r] = source[r]

    by_block[...] = jnp.zeros_like(by_block)
    for r in range(ROWS):
        rows = source[r]
        for b in range(16):
            by_block[b, pl.ds(r, 1), :] = rows[b : b + 1]

    row = lax.broadcasted_iota(jnp.int32, (48, ROWS * LANES), 0) & 15
    spread = jnp.where(row == lax.broadcasted_iota(jnp.int32, (48, ROWS * LANES), 1) >> 7, 1.0, 0.0)
    spread = spread.astype(jnp.bfloat16)

    def widen(b, _):
        rows = jnp.concatenate([part.astype(jnp.float32) for part in three_parts(by_block[b])], axis=0)
        wide = mm(rows.T.astype(jnp.bfloat16), spread)
        for r in range(ROWS):
            own_wide[b, r] = wide[:, r * LANES : (r + 1) * LANES]
        return 0

    lax.fori_loop(0, 16, widen, 0, unroll=4)

    arrived(pool, 2, 4)
    for step in (-1, 1):
        for p in (0, 2):
            pass_on(pool.at[p * 3 + 1], p, 1 - step, "gy", me_y, ny, step, 5)

    lane = lax.broadcasted_iota(jnp.int32, (8, LANES), 1)
    freq_z = me_x * 8 + (lane >> 4)
    freq_x = me_y * 16 + (lane & 15)

    def wave_of(index):
        sine = 2.0 * jnp.sin(index.astype(jnp.float32) * (math.pi / 256.0))
        return sine * sine

    wave_x, wave_z = wave_of(freq_x), wave_of(freq_z)
    both = wave_x + wave_z
    product = 2.0 / (1.0 - nu_copper) * wave_x * wave_z
    corner = (freq_x == 0) & (freq_z == 0)
    for i in range(32):
        total = both + wave[pl.ds(i * 8, 8), :]
        if i == 0:
            total = jnp.where(corner & (lax.broadcasted_iota(jnp.int32, (8, LANES), 0) == 0), 1.0, total)
        inverse = 1.0 / total
        gain[pl.ds(i * 8, 8), :] = (-2.0 / 256.0**3) * (1.0 - both * inverse + product * inverse * inverse)

    spot = ((place >> 7) & 1) * 128 + ((place >> 8) & 15) * 8 + (place >> 12)
    for b in range(16):
        want = jnp.broadcast_to(spot[b : b + 1], (256, LANES))
        at = lax.broadcasted_iota(jnp.int32, (256, LANES), 0)
        hot[:, b * LANES : (b + 1) * LANES] = jnp.where(want == at, 1.0, 0.0).astype(jnp.bfloat16)

    def pair_block(b, _):
        for n in range(8):
            partner = pair_ref[n, b]
            device = partner >> 4
            slot = partner & 15
            shift = {0: (lax.div(device, 3) - 1) * 8, 1: (lax.rem(device, 3) - 1) * 16}
            for r in range(ROWS):
                far = pool[device, r, pl.ds(slot, 1), :]
                if r in shift:
                    far = far + shift[r].astype(jnp.float32)
                far_wide[n, r] = jnp.broadcast_to(far, (8, LANES))

        def tile(i, _):
            rows = pl.ds(pl.multiple_of(i * 8, 8), 8)
            own = [own_wide[b, r, rows, :] for r in range(ROWS)]
            triple = [3.0 * own[3 + k] for k in range(3)]
            total = [jnp.zeros((8, LANES), jnp.float32) for _ in range(3)]
            for n in range(8):
                far = [far_wide[n, r] for r in range(ROWS)]
                delta = [own[k] - far[k] for k in range(3)]
                square = (delta[0] * delta[0] + core_sq) + (delta[1] * delta[1] + delta[2] * delta[2])
                inverse = lax.rsqrt(square)
                inv_two = inverse * inverse
                inv_three = inv_two * inverse
                burg_dot = own[3] * far[3] + own[4] * far[4] + own[5] * far[5]
                line_dot = own[6] * far[6] + own[7] * far[7] + own[8] * far[8]
                burg_own = triple[0] * delta[0] + triple[1] * delta[1] + triple[2] * delta[2]
                burg_far = far[3] * delta[0] + far[4] * delta[1] + far[5] * delta[2]
                weight = (line_dot * inv_three) * (burg_dot - (burg_own * burg_far) * inv_two)
                total = [total[k] + weight * delta[k] for k in range(3)]
            for k in range(3):
                sums[b, k, rows, :] = total[k]
            return 0

        lax.fori_loop(0, 16, tile, 0)
        return 0

    def pair_blocks(first, end):
        lax.fori_loop(first, end, pair_block, 0)
        column = lax.broadcasted_iota(jnp.int32, (2 * LANES, LANES), 1)
        have = pull[...]
        for b in range(first, end):
            for k in range(3):
                pick = jnp.where(column == k * 16 + b, 1.0, 0.0).astype(jnp.bfloat16)
                have = have + mm(jnp.concatenate(parts(sums[b, k]), axis=1), pick)
        pull[...] = have

    pull[...] = jnp.zeros_like(pull)

    arrived(recv1, nx - 1, 0)
    held = recv1[...].reshape(256, LANES)
    along_x = times_table(held.T, tab)
    for h in range(2):
        mid_a[h] = along_x[:, h * LANES : (h + 1) * LANES]
    for h in range(2):
        for s in range(2):
            tiles = [mid_a[h, pl.ds(s * 64 + c, 8, stride=8), :] for c in range(8)]
            for j, tile in enumerate(swap_blocks(tiles, 16)):
                send2[h * 8 + j, s * 8 : s * 8 + 8, :] = tile
    exchange("gy", me_y, ny, send2, recv2, 1)

    arrived(pool, 6, 5)
    pair_blocks(0, CUT[0])

    arrived(recv2, ny - 1, 1)
    spectrum = table_times(tab, recv2[...].reshape(256, LANES)) * gain[...]
    send3[...] = table_times(tab, spectrum).reshape(16, 16, LANES)
    exchange("gy", me_y, ny, send3, recv3, 2)
    pair_blocks(CUT[0], CUT[1])

    arrived(recv3, ny - 1, 2)
    for h in range(2):
        for s in range(2):
            tiles = [recv3[h * 8 + j, s * 8 : s * 8 + 8, :] for j in range(8)]
            for c, tile in enumerate(swap_blocks(tiles, 16)):
                mid_b[h, pl.ds(s * 64 + c, 8, stride=8), :] = tile
    back_x = jnp.concatenate([mid_b[0], mid_b[1]], axis=1).T
    send4[...] = table_times(tab, back_x).reshape(32, 8, LANES)
    exchange("gx", me_x, nx, send4, recv4, 3)
    pair_blocks(CUT[1], 16)

    arrived(recv4, nx - 1, 3)
    halves = []
    for h in range(2):
        tiles = [recv4[h * 16 + j] for j in range(16)]
        halves.append(jnp.concatenate(swap_blocks(tiles, 8), axis=0))
    final = times_table(jnp.concatenate(halves, axis=1), tab)
    for h in range(2):
        for y in range(16):
            stress[pl.ds(h * 128 + y, 8, stride=16), :] = final[y * 8 : y * 8 + 8, h * LANES : (h + 1) * LANES]
    tall = jnp.concatenate([final[:, :LANES], final[:, LANES:]], axis=0).T
    high, low = parts(tall)
    depth = place & 127
    tau_rows = []
    for b in range(16):
        picked = hot[:, b * LANES : (b + 1) * LANES]
        lines_b = mm(high, picked) + mm(low, picked)
        at = lax.broadcasted_iota(jnp.int32, (LANES, LANES), 0)
        chosen = jnp.where(at == jnp.broadcast_to(depth[b : b + 1], (LANES, LANES)), lines_b, 0.0)
        tau_rows.append(jnp.sum(chosen, axis=0, keepdims=True))
    tau = jnp.concatenate(tau_rows, axis=0)
    pulled = pull[...].T
    burgers = [source[3 + k] for k in range(3)]
    tangent = [source[6 + k] for k in range(3)]
    for k in range(3):
        k1, k2 = (k + 1) % 3, (k + 2) % 3
        glide = burgers[k1] * tangent[k2] - burgers[k2] * tangent[k1]
        force[k] = pair_scale * pulled[k * 16 : k * 16 + 16] + tau * glide
    left(send1, nx - 1, 0)
    left(send2, ny - 1, 1)
    left(send3, ny - 1, 2)
    left(send4, nx - 1, 3)
    left(pool, 8, 4)


def per_device(nx, ny, eigen, seg_vec, seg_off, seg_cell, blk_count, pair_list):
    f32, bf16 = jnp.float32, jnp.bfloat16
    tab = jnp.asarray(cas_table(256))
    sines = 2.0 * np.sin(np.arange(256) * (math.pi / 256.0))
    wave = jnp.asarray(np.repeat((sines * sines).astype(np.float32)[:, None], LANES, axis=1))
    hbm = pl.BlockSpec(memory_space=pltpu.HBM)
    out = pl.BlockSpec(memory_space=pltpu.VMEM)
    vmem = pltpu.VMEM
    stress, force = pl.pallas_call(
        functools.partial(kernel, nx, ny),
        out_shape=(
            vmem((256, LANES), f32),
            vmem((3, 16, LANES), f32),
        ),
        in_specs=[hbm] * 8,
        out_specs=(out, out),
        scratch_shapes=[
            vmem((2, 128, LANES), f32),
            vmem((6, 16, LANES), f32),
            vmem((3, 16, LANES), f32),
            vmem((16, LANES), jnp.int32),
            pltpu.SMEM((1, 16), jnp.int32),
            pltpu.SMEM((8, 16), jnp.int32),
            vmem((2, 256, 256), bf16),
            vmem((256, LANES), f32),
            vmem((32, 8, LANES), f32),
            vmem((32, 8, LANES), f32),
            vmem((16, 16, LANES), f32),
            vmem((16, 16, LANES), f32),
            vmem((16, 16, LANES), f32),
            vmem((16, 16, LANES), f32),
            vmem((32, 8, LANES), f32),
            vmem((32, 8, LANES), f32),
            vmem((2, 128, LANES), f32),
            vmem((2, 128, LANES), f32),
            vmem((256, LANES), f32),
            vmem((ROWS, 16, LANES), f32),
            vmem((9, ROWS, 16, LANES), f32),
            vmem((16, 16, LANES), f32),
            vmem((16, ROWS, LANES, LANES), f32),
            vmem((8, ROWS, 8, LANES), f32),
            vmem((16, 3, LANES, LANES), f32),
            vmem((LANES, LANES), f32),
            vmem((256, 2048), bf16),
            pltpu.SemaphoreType.DMA((9,)),
            pltpu.SemaphoreType.DMA((5,)),
            pltpu.SemaphoreType.DMA((6,)),
        ],
        compiler_params=pltpu.CompilerParams(
            collective_id=0, has_side_effects=True, vmem_limit_bytes=60 * 1024 * 1024
        ),
    )(
        eigen.reshape(128, 256),
        seg_vec.reshape(6, 16, LANES),
        seg_off.reshape(3, 16, LANES),
        seg_cell.reshape(16, LANES),
        blk_count.reshape(1, 16),
        pair_list.reshape(16, 8).T,
        tab,
        wave,
    )
    stress = jnp.concatenate([stress[:128], stress[128:]], axis=1)
    return stress.reshape(8, 16, 256), force.reshape(3, 1, 1, 2048)


def solution(mesh):
    return jax.shard_map(
        functools.partial(per_device, mesh.shape["gx"], mesh.shape["gy"]),
        mesh=mesh,
        in_specs=(
            P("gx", "gy", None),
            P(None, "gx", "gy", None),
            P(None, "gx", "gy", None),
            P("gx", "gy", None),
            P("gx", "gy", None),
            P("gx", "gy", None, None),
        ),
        out_specs=(P("gx", "gy", None), P(None, "gx", "gy", None)),
        check_vma=False,
    )
```

```python
import functools
import math

import jax
import jax.numpy as jnp
import ml_dtypes
import numpy as np
from jax import lax
from jax.experimental import pallas as pl
from jax.experimental.pallas import tpu as pltpu
from jax.sharding import PartitionSpec as P

nu_copper = 0.34
core_sq = 4.0
pair_scale = 4.0

MESH = pl.DeviceIdType.MESH
ROWS = 9
LANES = 128
CUT = (5, 10)


def cas_table(length):
    steps = np.arange(length)
    angle = (steps[:, None] * steps[None, :] % length) * (2.0 * math.pi / length)
    table = np.cos(angle) + np.sin(angle)
    high = table.astype(ml_dtypes.bfloat16)
    low = (table - high.astype(np.float64)).astype(ml_dtypes.bfloat16)
    return np.stack([high, low])


def parts(x):
    high = x.astype(jnp.bfloat16)
    return high, (x - high.astype(jnp.float32)).astype(jnp.bfloat16)


def three_parts(x):
    high = x.astype(jnp.bfloat16)
    rest = x - high.astype(jnp.float32)
    return high, *parts(rest)


def mm(a, b):
    return jnp.dot(a, b, preferred_element_type=jnp.float32)


def times_table(x, tab):
    high, low = parts(x)
    return mm(high, tab[0]) + (mm(low, tab[0]) + mm(high, tab[1]))


def table_times(tab, x):
    high, low = parts(x)
    return mm(tab[0], high) + (mm(tab[0], low) + mm(tab[1], high))


def swap_blocks(tiles, width):
    count = len(tiles)
    lane = lax.broadcasted_iota(jnp.int32, (8, LANES), 1) // width
    tiles = list(tiles)
    bit = 1
    while bit < count:
        keep = (lane & bit) == 0
        shift = bit * width
        for i in range(count):
            if i & bit:
                continue
            a, c = tiles[i], tiles[i | bit]
            tiles[i] = jnp.where(keep, a, pltpu.roll(c, shift, 1))
            tiles[i | bit] = jnp.where(keep, pltpu.roll(a, LANES - shift, 1), c)
        bit *= 2
    return tiles


def kernel(
    nx, ny, eigen_hbm, vec_hbm, off_hbm, cell_hbm, count_hbm, pair_hbm, tab_hbm, wave_hbm,
    stress, force,
    eigen, vec, off, cell, count_ref, pair_ref, tab, wave, send1, recv1, send2, recv2, send3, recv3, send4, recv4,
    mid_a, mid_b, gain, source, pool, by_block, own_wide, far_wide, sums, pull, hot,
    load_sem, send_sem, recv_sem,
):
    me_x = lax.axis_index("gx")
    me_y = lax.axis_index("gy")

    def swing(k, middle):
        return middle + ((k + 1) >> 1) * (1 - 2 * (k & 1))

    def peer_of(me, count, i):
        inner = count // 8
        outer = ((me // inner) + swing(i // inner, 4)) & 7
        return outer * inner + ((me + swing(i % inner, inner // 2)) & (inner - 1))

    loads = [
        pltpu.make_async_copy(src, dst, load_sem.at[n])
        for n, (src, dst) in enumerate(
            (
                (eigen_hbm.at[:, pl.ds(0, LANES)], eigen.at[0]),
                (eigen_hbm.at[:, pl.ds(LANES, LANES)], eigen.at[1]),
                (tab_hbm, tab),
                (vec_hbm, vec),
                (off_hbm, off),
                (cell_hbm, cell),
                (count_hbm, count_ref),
                (pair_hbm, pair_ref),
                (wave_hbm, wave),
            )
        )
    ]
    for load in loads:
        load.start()

    barrier = pltpu.get_barrier_semaphore()

    for axis, me, count in (("gx", me_x, nx), ("gy", me_y, ny)):
        for i in range(count - 1):
            pl.semaphore_signal(
                barrier, inc=1, device_id={axis: peer_of(me, count, i)}, device_id_type=MESH
            )

    for load in loads[3:]:
        load.wait()
    row_id = lax.broadcasted_iota(jnp.int32, (16, LANES), 0)
    lane_id = lax.broadcasted_iota(jnp.int32, (16, LANES), 1)
    counts = jnp.zeros((16, LANES), jnp.int32)
    for b in range(16):
        counts = jnp.where(row_id == b, count_ref[0, b], counts)
    live = jnp.where(lane_id < counts, 1.0, 0.0)
    place = cell[...]
    spots = (place >> 12, (place >> 8) & 15, place & 255)
    for k in range(3):
        source[k] = spots[k].astype(jnp.float32) + off[k]
        source[3 + k] = vec[k] * live
        source[6 + k] = vec[3 + k]
    for load in loads[:3]:
        load.wait()

    lines = jnp.concatenate(
        [
            jnp.concatenate([eigen[h, pl.ds(y, 8, stride=16), :] for h in range(2)], axis=1)
            for y in range(16)
        ],
        axis=0,
    )
    zeta = times_table(lines, tab)
    for h in range(2):
        tiles = [zeta[y * 8 : y * 8 + 8, h * LANES : (h + 1) * LANES] for y in range(16)]
        for j, tile in enumerate(swap_blocks(tiles, 8)):
            send1[h * 16 + j] = tile

    by_block[...] = jnp.zeros_like(by_block)
    for r in range(ROWS):
        rows = source[r]
        for b in range(16):
            by_block[b, pl.ds(r, 1), :] = rows[b : b + 1]

    row = lax.broadcasted_iota(jnp.int32, (48, ROWS * LANES), 0) & 15
    spread = jnp.where(row == lax.broadcasted_iota(jnp.int32, (48, ROWS * LANES), 1) >> 7, 1.0, 0.0)
    spread = spread.astype(jnp.bfloat16)

    def widen(b, _):
        rows = jnp.concatenate([part.astype(jnp.float32) for part in three_parts(by_block[b])], axis=0)
        wide = mm(rows.T.astype(jnp.bfloat16), spread)
        for r in range(ROWS):
            own_wide[b, r] = wide[:, r * LANES : (r + 1) * LANES]
        return 0

    lax.fori_loop(0, 16, widen, 0, unroll=4)

    pl.semaphore_wait(barrier, nx - 1 + ny - 1)

    def exchange(axis, me, count, send, recv, stage):
        for i in range(count - 1):
            peer = peer_of(me, count, i)
            pltpu.make_async_remote_copy(
                src_ref=send.at[peer], dst_ref=recv.at[me], send_sem=send_sem.at[stage],
                recv_sem=recv_sem.at[stage], device_id={axis: peer}, device_id_type=MESH,
            ).start()
        recv[me] = send[me]

    def arrived(buffer, count, stage):
        whole = buffer.at[pl.ds(0, count)]
        pltpu.make_async_copy(whole, whole, recv_sem.at[stage]).wait()

    def left(buffer, count, stage):
        whole = buffer.at[pl.ds(0, count)]
        pltpu.make_async_copy(whole, whole, send_sem.at[stage]).wait()

    def pass_on(column, p, q, axis, me, count, step, stage):
        pltpu.make_async_remote_copy(
            src_ref=column, dst_ref=pool.at[p * 3 + q], send_sem=send_sem.at[4], recv_sem=recv_sem.at[stage],
            device_id={axis: (me + step) & (count - 1)}, device_id_type=MESH,
        ).start()

    for step in (-1, 1):
        pass_on(source, 1, 1 - step, "gy", me_y, ny, step, 4)
    for step in (-1, 1):
        pass_on(source, 1 - step, 1, "gx", me_x, nx, step, 5)
    exchange("gx", me_x, nx, send1, recv1, 0)

    for r in range(ROWS):
        pool[4, r] = source[r]

    arrived(pool, 2, 4)
    for step in (-1, 1):
        for q in (0, 2):
            pass_on(pool.at[3 + q], 1 - step, q, "gx", me_x, nx, step, 5)

    lane = lax.broadcasted_iota(jnp.int32, (8, LANES), 1)
    freq_z = me_x * 8 + (lane >> 4)
    freq_x = me_y * 16 + (lane & 15)

    def wave_of(index):
        sine = 2.0 * jnp.sin(index.astype(jnp.float32) * (math.pi / 256.0))
        return sine * sine

    wave_x, wave_z = wave_of(freq_x), wave_of(freq_z)
    both = wave_x + wave_z
    product = 2.0 / (1.0 - nu_copper) * wave_x * wave_z
    corner = (freq_x == 0) & (freq_z == 0)
    for i in range(32):
        total = both + wave[pl.ds(i * 8, 8), :]
        if i == 0:
            total = jnp.where(corner & (lax.broadcasted_iota(jnp.int32, (8, LANES), 0) == 0), 1.0, total)
        inverse = 1.0 / total
        gain[pl.ds(i * 8, 8), :] = (-2.0 / 256.0**3) * (1.0 - both * inverse + product * inverse * inverse)

    spot = ((place >> 7) & 1) * 128 + ((place >> 8) & 15) * 8 + (place >> 12)
    for b in range(16):
        want = jnp.broadcast_to(spot[b : b + 1], (256, LANES))
        at = lax.broadcasted_iota(jnp.int32, (256, LANES), 0)
        hot[:, b * LANES : (b + 1) * LANES] = jnp.where(want == at, 1.0, 0.0).astype(jnp.bfloat16)

    def pair_block(b, _):
        for n in range(8):
            partner = pair_ref[n, b]
            device = partner >> 4
            slot = partner & 15
            shift = {0: (lax.div(device, 3) - 1) * 8, 1: (lax.rem(device, 3) - 1) * 16}
            for r in range(ROWS):
                far = pool[device, r, pl.ds(slot, 1), :]
                if r in shift:
                    far = far + shift[r].astype(jnp.float32)
                far_wide[n, r] = jnp.broadcast_to(far, (8, LANES))

        def tile(i, _):
            rows = pl.ds(pl.multiple_of(i * 8, 8), 8)
            own = [own_wide[b, r, rows, :] for r in range(ROWS)]
            triple = [3.0 * own[3 + k] for k in range(3)]
            total = [jnp.zeros((8, LANES), jnp.float32) for _ in range(3)]
            for n in range(8):
                far = [far_wide[n, r] for r in range(ROWS)]
                delta = [own[k] - far[k] for k in range(3)]
                square = (delta[0] * delta[0] + core_sq) + (delta[1] * delta[1] + delta[2] * delta[2])
                inverse = lax.rsqrt(square)
                inv_two = inverse * inverse
                inv_three = inv_two * inverse
                burg_dot = own[3] * far[3] + own[4] * far[4] + own[5] * far[5]
                line_dot = own[6] * far[6] + own[7] * far[7] + own[8] * far[8]
                burg_own = triple[0] * delta[0] + triple[1] * delta[1] + triple[2] * delta[2]
                burg_far = far[3] * delta[0] + far[4] * delta[1] + far[5] * delta[2]
                weight = (line_dot * inv_three) * (burg_dot - (burg_own * burg_far) * inv_two)
                total = [total[k] + weight * delta[k] for k in range(3)]
            for k in range(3):
                sums[b, k, rows, :] = total[k]
            return 0

        lax.fori_loop(0, 16, tile, 0, unroll=4)
        return 0

    def pair_blocks(first, end):
        lax.fori_loop(first, end, pair_block, 0)
        high, low = parts(sums[first:end].reshape((end - first) * 3 * LANES, LANES))
        ones = jnp.ones((2 * LANES, LANES), jnp.bfloat16)
        added = mm(jnp.concatenate([high, low], axis=1), ones)
        column = lax.broadcasted_iota(jnp.int32, (LANES, LANES), 1)
        have = pull[...]
        for n in range((end - first) * 3):
            spot = (n % 3) * 16 + first + n // 3
            have = jnp.where(column == spot, added[n * LANES : (n + 1) * LANES], have)
        pull[...] = have

    pull[...] = jnp.zeros_like(pull)

    arrived(recv1, nx - 1, 0)
    held = recv1[...].reshape(256, LANES)
    along_x = times_table(held.T, tab)
    for h in range(2):
        mid_a[h] = along_x[:, h * LANES : (h + 1) * LANES]
    for h in range(2):
        for s in range(2):
            tiles = [mid_a[h, pl.ds(s * 64 + c, 8, stride=8), :] for c in range(8)]
            for j, tile in enumerate(swap_blocks(tiles, 16)):
                send2[h * 8 + j, s * 8 : s * 8 + 8, :] = tile
    exchange("gy", me_y, ny, send2, recv2, 1)

    arrived(pool, 6, 5)
    pair_blocks(0, CUT[0])

    arrived(recv2, ny - 1, 1)
    spectrum = table_times(tab, recv2[...].reshape(256, LANES)) * gain[...]
    send3[...] = table_times(tab, spectrum).reshape(16, 16, LANES)
    exchange("gy", me_y, ny, send3, recv3, 2)
    pair_blocks(CUT[0], CUT[1])

    arrived(recv3, ny - 1, 2)
    for h in range(2):
        for s in range(2):
            tiles = [recv3[h * 8 + j, s * 8 : s * 8 + 8, :] for j in range(8)]
            for c, tile in enumerate(swap_blocks(tiles, 16)):
                mid_b[h, pl.ds(s * 64 + c, 8, stride=8), :] = tile
    back_x = jnp.concatenate([mid_b[0], mid_b[1]], axis=1).T
    send4[...] = table_times(tab, back_x).reshape(32, 8, LANES)
    exchange("gx", me_x, nx, send4, recv4, 3)
    pair_blocks(CUT[1], 16)

    arrived(recv4, nx - 1, 3)
    halves = []
    for h in range(2):
        tiles = [recv4[h * 16 + j] for j in range(16)]
        halves.append(jnp.concatenate(swap_blocks(tiles, 8), axis=0))
    final = times_table(jnp.concatenate(halves, axis=1), tab)
    for h in range(2):
        for y in range(16):
            stress[pl.ds(h * 128 + y, 8, stride=16), :] = final[y * 8 : y * 8 + 8, h * LANES : (h + 1) * LANES]
    tall = jnp.concatenate([final[:, :LANES], final[:, LANES:]], axis=0).T
    high, low = parts(tall)
    depth = place & 127
    tau_rows = []
    for b in range(16):
        picked = hot[:, b * LANES : (b + 1) * LANES]
        lines_b = mm(high, picked) + mm(low, picked)
        at = lax.broadcasted_iota(jnp.int32, (LANES, LANES), 0)
        chosen = jnp.where(at == jnp.broadcast_to(depth[b : b + 1], (LANES, LANES)), lines_b, 0.0)
        tau_rows.append(jnp.sum(chosen, axis=0, keepdims=True))
    tau = jnp.concatenate(tau_rows, axis=0)
    pulled = pull[...].T
    burgers = [source[3 + k] for k in range(3)]
    tangent = [source[6 + k] for k in range(3)]
    for k in range(3):
        k1, k2 = (k + 1) % 3, (k + 2) % 3
        glide = burgers[k1] * tangent[k2] - burgers[k2] * tangent[k1]
        force[k] = pair_scale * pulled[k * 16 : k * 16 + 16] + tau * glide
    left(send1, nx - 1, 0)
    left(send2, ny - 1, 1)
    left(send3, ny - 1, 2)
    left(send4, nx - 1, 3)
    left(pool, 8, 4)


def per_device(nx, ny, eigen, seg_vec, seg_off, seg_cell, blk_count, pair_list):
    f32, bf16 = jnp.float32, jnp.bfloat16
    tab = jnp.asarray(cas_table(256))
    sines = 2.0 * np.sin(np.arange(256) * (math.pi / 256.0))
    wave = jnp.asarray(np.repeat((sines * sines).astype(np.float32)[:, None], LANES, axis=1))
    hbm = pl.BlockSpec(memory_space=pltpu.HBM)
    out = pl.BlockSpec(memory_space=pltpu.VMEM)
    vmem = pltpu.VMEM
    stress, force = pl.pallas_call(
        functools.partial(kernel, nx, ny),
        out_shape=(
            vmem((256, LANES), f32),
            vmem((3, 16, LANES), f32),
        ),
        in_specs=[hbm] * 8,
        out_specs=(out, out),
        scratch_shapes=[
            vmem((2, 128, LANES), f32),
            vmem((6, 16, LANES), f32),
            vmem((3, 16, LANES), f32),
            vmem((16, LANES), jnp.int32),
            pltpu.SMEM((1, 16), jnp.int32),
            pltpu.SMEM((8, 16), jnp.int32),
            vmem((2, 256, 256), bf16),
            vmem((256, LANES), f32),
            vmem((32, 8, LANES), f32),
            vmem((32, 8, LANES), f32),
            vmem((16, 16, LANES), f32),
            vmem((16, 16, LANES), f32),
            vmem((16, 16, LANES), f32),
            vmem((16, 16, LANES), f32),
            vmem((32, 8, LANES), f32),
            vmem((32, 8, LANES), f32),
            vmem((2, 128, LANES), f32),
            vmem((2, 128, LANES), f32),
            vmem((256, LANES), f32),
            vmem((ROWS, 16, LANES), f32),
            vmem((9, ROWS, 16, LANES), f32),
            vmem((16, 16, LANES), f32),
            vmem((16, ROWS, LANES, LANES), f32),
            vmem((8, ROWS, 8, LANES), f32),
            vmem((16, 3, LANES, LANES), f32),
            vmem((LANES, LANES), f32),
            vmem((256, 2048), bf16),
            pltpu.SemaphoreType.DMA((9,)),
            pltpu.SemaphoreType.DMA((5,)),
            pltpu.SemaphoreType.DMA((6,)),
        ],
        compiler_params=pltpu.CompilerParams(
            collective_id=0, has_side_effects=True, vmem_limit_bytes=60 * 1024 * 1024
        ),
    )(
        eigen.reshape(128, 256),
        seg_vec.reshape(6, 16, LANES),
        seg_off.reshape(3, 16, LANES),
        seg_cell.reshape(16, LANES),
        blk_count.reshape(1, 16),
        pair_list.reshape(16, 8).T,
        tab,
        wave,
    )
    stress = jnp.concatenate([stress[:128], stress[128:]], axis=1)
    return stress.reshape(8, 16, 256), force.reshape(3, 1, 1, 2048)


def solution(mesh):
    return jax.shard_map(
        functools.partial(per_device, mesh.shape["gx"], mesh.shape["gy"]),
        mesh=mesh,
        in_specs=(
            P("gx", "gy", None),
            P(None, "gx", "gy", None),
            P(None, "gx", "gy", None),
            P("gx", "gy", None),
            P("gx", "gy", None),
            P("gx", "gy", None, None),
        ),
        out_specs=(P("gx", "gy", None), P(None, "gx", "gy", None)),
        check_vma=False,
    )
```

```python
import functools
import math

import jax
import jax.numpy as jnp
import ml_dtypes
import numpy as np
from jax import lax
from jax.experimental import pallas as pl
from jax.experimental.pallas import tpu as pltpu
from jax.sharding import PartitionSpec as P

nu_copper = 0.34
core_sq = 4.0
pair_scale = 4.0

MESH = pl.DeviceIdType.MESH
ROWS = 9
LANES = 128
CUT = (5, 10)


def cas_table(length):
    steps = np.arange(length)
    angle = (steps[:, None] * steps[None, :] % length) * (2.0 * math.pi / length)
    table = np.cos(angle) + np.sin(angle)
    high = table.astype(ml_dtypes.bfloat16)
    low = (table - high.astype(np.float64)).astype(ml_dtypes.bfloat16)
    return np.stack([high, low])


def parts(x):
    high = x.astype(jnp.bfloat16)
    return high, (x - high.astype(jnp.float32)).astype(jnp.bfloat16)


def three_parts(x):
    high = x.astype(jnp.bfloat16)
    rest = x - high.astype(jnp.float32)
    return high, *parts(rest)


def mm(a, b):
    return jnp.dot(a, b, preferred_element_type=jnp.float32)


def times_table(x, tab):
    high, low = parts(x)
    return mm(high, tab[0]) + (mm(low, tab[0]) + mm(high, tab[1]))


def table_times(tab, x):
    high, low = parts(x)
    return mm(tab[0], high) + (mm(tab[0], low) + mm(tab[1], high))


def swap_blocks(tiles, width):
    count = len(tiles)
    lane = lax.broadcasted_iota(jnp.int32, (8, LANES), 1) // width
    tiles = list(tiles)
    bit = 1
    while bit < count:
        keep = (lane & bit) == 0
        shift = bit * width
        for i in range(count):
            if i & bit:
                continue
            a, c = tiles[i], tiles[i | bit]
            tiles[i] = jnp.where(keep, a, pltpu.roll(c, shift, 1))
            tiles[i | bit] = jnp.where(keep, pltpu.roll(a, LANES - shift, 1), c)
        bit *= 2
    return tiles


def kernel(
    nx, ny, eigen_hbm, vec_hbm, off_hbm, cell_hbm, count_hbm, pair_hbm, tab_hbm, wave_hbm,
    stress, force,
    eigen, vec, off, cell, count_ref, pair_ref, tab, wave, send1, recv1, send2, recv2, send3, recv3, send4, recv4,
    mid_a, mid_b, gain, source, pool, by_block, own_wide, far_wide, sums, pull, hot,
    load_sem, send_sem, recv_sem,
):
    me_x = lax.axis_index("gx")
    me_y = lax.axis_index("gy")

    def swing(k, middle):
        return middle + ((k + 1) >> 1) * (1 - 2 * (k & 1))

    def peer_of(me, count, i):
        inner = count // 8
        outer = ((me // inner) + swing(i // inner, 4)) & 7
        return outer * inner + ((me + swing(i % inner, inner // 2)) & (inner - 1))

    loads = [
        pltpu.make_async_copy(src, dst, load_sem.at[n])
        for n, (src, dst) in enumerate(
            (
                (eigen_hbm.at[:, pl.ds(0, LANES)], eigen.at[0]),
                (eigen_hbm.at[:, pl.ds(LANES, LANES)], eigen.at[1]),
                (tab_hbm, tab),
                (vec_hbm, vec),
                (off_hbm, off),
                (cell_hbm, cell),
                (count_hbm, count_ref),
                (pair_hbm, pair_ref),
                (wave_hbm, wave),
            )
        )
    ]
    for load in loads:
        load.start()

    barrier = pltpu.get_barrier_semaphore()

    for axis, me, count in (("gx", me_x, nx), ("gy", me_y, ny)):
        for i in range(count - 1):
            pl.semaphore_signal(
                barrier, inc=1, device_id={axis: peer_of(me, count, i)}, device_id_type=MESH
            )

    for load in loads[3:]:
        load.wait()
    row_id = lax.broadcasted_iota(jnp.int32, (16, LANES), 0)
    lane_id = lax.broadcasted_iota(jnp.int32, (16, LANES), 1)
    counts = jnp.zeros((16, LANES), jnp.int32)
    for b in range(16):
        counts = jnp.where(row_id == b, count_ref[0, b], counts)
    live = jnp.where(lane_id < counts, 1.0, 0.0)
    place = cell[...]
    spots = (place >> 12, (place >> 8) & 15, place & 255)
    for k in range(3):
        source[k] = spots[k].astype(jnp.float32) + off[k]
        source[3 + k] = vec[k] * live
        source[6 + k] = vec[3 + k]
    for load in loads[:3]:
        load.wait()

    lines = jnp.concatenate(
        [
            jnp.concatenate([eigen[h, pl.ds(y, 8, stride=16), :] for h in range(2)], axis=1)
            for y in range(16)
        ],
        axis=0,
    )
    zeta = times_table(lines, tab)
    for h in range(2):
        tiles = [zeta[y * 8 : y * 8 + 8, h * LANES : (h + 1) * LANES] for y in range(16)]
        for j, tile in enumerate(swap_blocks(tiles, 8)):
            send1[h * 16 + j] = tile

    by_block[...] = jnp.zeros_like(by_block)
    for r in range(ROWS):
        rows = source[r]
        for b in range(16):
            by_block[b, pl.ds(r, 1), :] = rows[b : b + 1]

    row = lax.broadcasted_iota(jnp.int32, (48, ROWS * LANES), 0) & 15
    spread = jnp.where(row == lax.broadcasted_iota(jnp.int32, (48, ROWS * LANES), 1) >> 7, 1.0, 0.0)
    spread = spread.astype(jnp.bfloat16)

    def widen(b, _):
        rows = jnp.concatenate([part.astype(jnp.float32) for part in three_parts(by_block[b])], axis=0)
        wide = mm(rows.T.astype(jnp.bfloat16), spread)
        for r in range(ROWS):
            own_wide[b, r] = wide[:, r * LANES : (r + 1) * LANES]
        return 0

    lax.fori_loop(0, 16, widen, 0, unroll=4)

    pl.semaphore_wait(barrier, nx - 1 + ny - 1)

    def exchange(axis, me, count, send, recv, stage):
        for i in range(count - 1):
            peer = peer_of(me, count, i)
            pltpu.make_async_remote_copy(
                src_ref=send.at[peer], dst_ref=recv.at[me], send_sem=send_sem.at[stage],
                recv_sem=recv_sem.at[stage], device_id={axis: peer}, device_id_type=MESH,
            ).start()
        recv[me] = send[me]

    def arrived(buffer, count, stage):
        whole = buffer.at[pl.ds(0, count)]
        pltpu.make_async_copy(whole, whole, recv_sem.at[stage]).wait()

    def left(buffer, count, stage):
        whole = buffer.at[pl.ds(0, count)]
        pltpu.make_async_copy(whole, whole, send_sem.at[stage]).wait()

    def pass_on(column, p, q, axis, me, count, step, stage):
        pltpu.make_async_remote_copy(
            src_ref=column, dst_ref=pool.at[p * 3 + q], send_sem=send_sem.at[4], recv_sem=recv_sem.at[stage],
            device_id={axis: (me + step) & (count - 1)}, device_id_type=MESH,
        ).start()

    for step in (-1, 1):
        pass_on(source, 1, 1 - step, "gy", me_y, ny, step, 4 + (1 - step))
    for step in (-1, 1):
        pass_on(source, 1 - step, 1, "gx", me_x, nx, step, 5)
    exchange("gx", me_x, nx, send1, recv1, 0)

    for r in range(ROWS):
        pool[4, r] = source[r]

    def relay(q):
        arrived(pool, 1, 4 + q)
        for step in (-1, 1):
            pass_on(pool.at[3 + q], 1 - step, q, "gx", me_x, nx, step, 5)

    near = 2 - 2 * (me_y & 1)
    relay(near)
    relay(2 - near)

    lane = lax.broadcasted_iota(jnp.int32, (8, LANES), 1)
    freq_z = me_x * 8 + (lane >> 4)
    freq_x = me_y * 16 + (lane & 15)

    def wave_of(index):
        sine = 2.0 * jnp.sin(index.astype(jnp.float32) * (math.pi / 256.0))
        return sine * sine

    wave_x, wave_z = wave_of(freq_x), wave_of(freq_z)
    both = wave_x + wave_z
    product = 2.0 / (1.0 - nu_copper) * wave_x * wave_z
    corner = (freq_x == 0) & (freq_z == 0)
    for i in range(32):
        total = both + wave[pl.ds(i * 8, 8), :]
        if i == 0:
            total = jnp.where(corner & (lax.broadcasted_iota(jnp.int32, (8, LANES), 0) == 0), 1.0, total)
        inverse = 1.0 / total
        gain[pl.ds(i * 8, 8), :] = (-2.0 / 256.0**3) * (1.0 - both * inverse + product * inverse * inverse)

    spot = ((place >> 7) & 1) * 128 + ((place >> 8) & 15) * 8 + (place >> 12)
    for b in range(16):
        want = jnp.broadcast_to(spot[b : b + 1], (256, LANES))
        at = lax.broadcasted_iota(jnp.int32, (256, LANES), 0)
        hot[:, b * LANES : (b + 1) * LANES] = jnp.where(want == at, 1.0, 0.0).astype(jnp.bfloat16)

    def pair_block(b, _):
        for n in range(8):
            partner = pair_ref[n, b]
            device = partner >> 4
            slot = partner & 15
            shift = {0: (lax.div(device, 3) - 1) * 8, 1: (lax.rem(device, 3) - 1) * 16}
            for r in range(ROWS):
                far = pool[device, r, pl.ds(slot, 1), :]
                if r in shift:
                    far = far + shift[r].astype(jnp.float32)
                far_wide[n, r] = jnp.broadcast_to(far, (8, LANES))

        def tile(i, _):
            rows = pl.ds(pl.multiple_of(i * 8, 8), 8)
            own = [own_wide[b, r, rows, :] for r in range(ROWS)]
            triple = [3.0 * own[3 + k] for k in range(3)]
            total = [jnp.zeros((8, LANES), jnp.float32) for _ in range(3)]
            for n in range(8):
                far = [far_wide[n, r] for r in range(ROWS)]
                delta = [own[k] - far[k] for k in range(3)]
                square = (delta[0] * delta[0] + core_sq) + (delta[1] * delta[1] + delta[2] * delta[2])
                inverse = lax.rsqrt(square)
                inv_two = inverse * inverse
                inv_three = inv_two * inverse
                burg_dot = own[3] * far[3] + own[4] * far[4] + own[5] * far[5]
                line_dot = own[6] * far[6] + own[7] * far[7] + own[8] * far[8]
                burg_own = triple[0] * delta[0] + triple[1] * delta[1] + triple[2] * delta[2]
                burg_far = far[3] * delta[0] + far[4] * delta[1] + far[5] * delta[2]
                weight = (line_dot * inv_three) * (burg_dot - (burg_own * burg_far) * inv_two)
                total = [total[k] + weight * delta[k] for k in range(3)]
            for k in range(3):
                sums[b, k, rows, :] = total[k]
            return 0

        lax.fori_loop(0, 16, tile, 0, unroll=4)
        return 0

    def pair_blocks(first, end):
        lax.fori_loop(first, end, pair_block, 0)
        high, low = parts(sums[first:end].reshape((end - first) * 3 * LANES, LANES))
        ones = jnp.ones((2 * LANES, LANES), jnp.bfloat16)
        added = mm(jnp.concatenate([high, low], axis=1), ones)
        column = lax.broadcasted_iota(jnp.int32, (LANES, LANES), 1)
        have = pull[...]
        for n in range((end - first) * 3):
            spot = (n % 3) * 16 + first + n // 3
            have = jnp.where(column == spot, added[n * LANES : (n + 1) * LANES], have)
        pull[...] = have

    pull[...] = jnp.zeros_like(pull)

    arrived(recv1, nx - 1, 0)
    held = recv1[...].reshape(256, LANES)
    along_x = times_table(held.T, tab)
    for h in range(2):
        mid_a[h] = along_x[:, h * LANES : (h + 1) * LANES]
    for h in range(2):
        for s in range(2):
            tiles = [mid_a[h, pl.ds(s * 64 + c, 8, stride=8), :] for c in range(8)]
            for j, tile in enumerate(swap_blocks(tiles, 16)):
                send2[h * 8 + j, s * 8 : s * 8 + 8, :] = tile
    exchange("gy", me_y, ny, send2, recv2, 1)

    arrived(pool, 6, 5)
    pair_blocks(0, CUT[0])

    arrived(recv2, ny - 1, 1)
    spectrum = table_times(tab, recv2[...].reshape(256, LANES)) * gain[...]
    send3[...] = table_times(tab, spectrum).reshape(16, 16, LANES)
    exchange("gy", me_y, ny, send3, recv3, 2)
    pair_blocks(CUT[0], CUT[1])

    arrived(recv3, ny - 1, 2)
    for h in range(2):
        for s in range(2):
            tiles = [recv3[h * 8 + j, s * 8 : s * 8 + 8, :] for j in range(8)]
            for c, tile in enumerate(swap_blocks(tiles, 16)):
                mid_b[h, pl.ds(s * 64 + c, 8, stride=8), :] = tile
    back_x = jnp.concatenate([mid_b[0], mid_b[1]], axis=1).T
    send4[...] = table_times(tab, back_x).reshape(32, 8, LANES)
    exchange("gx", me_x, nx, send4, recv4, 3)
    pair_blocks(CUT[1], 16)

    arrived(recv4, nx - 1, 3)
    halves = []
    for h in range(2):
        tiles = [recv4[h * 16 + j] for j in range(16)]
        halves.append(jnp.concatenate(swap_blocks(tiles, 8), axis=0))
    final = times_table(jnp.concatenate(halves, axis=1), tab)
    for h in range(2):
        for y in range(16):
            stress[pl.ds(h * 128 + y, 8, stride=16), :] = final[y * 8 : y * 8 + 8, h * LANES : (h + 1) * LANES]
    tall = jnp.concatenate([final[:, :LANES], final[:, LANES:]], axis=0).T
    high, low = parts(tall)
    depth = place & 127
    tau_rows = []
    for b in range(16):
        picked = hot[:, b * LANES : (b + 1) * LANES]
        lines_b = mm(high, picked) + mm(low, picked)
        at = lax.broadcasted_iota(jnp.int32, (LANES, LANES), 0)
        chosen = jnp.where(at == jnp.broadcast_to(depth[b : b + 1], (LANES, LANES)), lines_b, 0.0)
        tau_rows.append(jnp.sum(chosen, axis=0, keepdims=True))
    tau = jnp.concatenate(tau_rows, axis=0)
    pulled = pull[...].T
    burgers = [source[3 + k] for k in range(3)]
    tangent = [source[6 + k] for k in range(3)]
    for k in range(3):
        k1, k2 = (k + 1) % 3, (k + 2) % 3
        glide = burgers[k1] * tangent[k2] - burgers[k2] * tangent[k1]
        force[k] = pair_scale * pulled[k * 16 : k * 16 + 16] + tau * glide
    left(send1, nx - 1, 0)
    left(send2, ny - 1, 1)
    left(send3, ny - 1, 2)
    left(send4, nx - 1, 3)
    left(pool, 8, 4)


def per_device(nx, ny, eigen, seg_vec, seg_off, seg_cell, blk_count, pair_list):
    f32, bf16 = jnp.float32, jnp.bfloat16
    tab = jnp.asarray(cas_table(256))
    sines = 2.0 * np.sin(np.arange(256) * (math.pi / 256.0))
    wave = jnp.asarray(np.repeat((sines * sines).astype(np.float32)[:, None], LANES, axis=1))
    hbm = pl.BlockSpec(memory_space=pltpu.HBM)
    out = pl.BlockSpec(memory_space=pltpu.VMEM)
    vmem = pltpu.VMEM
    stress, force = pl.pallas_call(
        functools.partial(kernel, nx, ny),
        out_shape=(
            vmem((256, LANES), f32),
            vmem((3, 16, LANES), f32),
        ),
        in_specs=[hbm] * 8,
        out_specs=(out, out),
        scratch_shapes=[
            vmem((2, 128, LANES), f32),
            vmem((6, 16, LANES), f32),
            vmem((3, 16, LANES), f32),
            vmem((16, LANES), jnp.int32),
            pltpu.SMEM((1, 16), jnp.int32),
            pltpu.SMEM((8, 16), jnp.int32),
            vmem((2, 256, 256), bf16),
            vmem((256, LANES), f32),
            vmem((32, 8, LANES), f32),
            vmem((32, 8, LANES), f32),
            vmem((16, 16, LANES), f32),
            vmem((16, 16, LANES), f32),
            vmem((16, 16, LANES), f32),
            vmem((16, 16, LANES), f32),
            vmem((32, 8, LANES), f32),
            vmem((32, 8, LANES), f32),
            vmem((2, 128, LANES), f32),
            vmem((2, 128, LANES), f32),
            vmem((256, LANES), f32),
            vmem((ROWS, 16, LANES), f32),
            vmem((9, ROWS, 16, LANES), f32),
            vmem((16, 16, LANES), f32),
            vmem((16, ROWS, LANES, LANES), f32),
            vmem((8, ROWS, 8, LANES), f32),
            vmem((16, 3, LANES, LANES), f32),
            vmem((LANES, LANES), f32),
            vmem((256, 2048), bf16),
            pltpu.SemaphoreType.DMA((9,)),
            pltpu.SemaphoreType.DMA((5,)),
            pltpu.SemaphoreType.DMA((7,)),
        ],
        compiler_params=pltpu.CompilerParams(
            collective_id=0, has_side_effects=True, vmem_limit_bytes=60 * 1024 * 1024
        ),
    )(
        eigen.reshape(128, 256),
        seg_vec.reshape(6, 16, LANES),
        seg_off.reshape(3, 16, LANES),
        seg_cell.reshape(16, LANES),
        blk_count.reshape(1, 16),
        pair_list.reshape(16, 8).T,
        tab,
        wave,
    )
    stress = jnp.concatenate([stress[:128], stress[128:]], axis=1)
    return stress.reshape(8, 16, 256), force.reshape(3, 1, 1, 2048)


def solution(mesh):
    return jax.shard_map(
        functools.partial(per_device, mesh.shape["gx"], mesh.shape["gy"]),
        mesh=mesh,
        in_specs=(
            P("gx", "gy", None),
            P(None, "gx", "gy", None),
            P(None, "gx", "gy", None),
            P("gx", "gy", None),
            P("gx", "gy", None),
            P("gx", "gy", None, None),
        ),
        out_specs=(P("gx", "gy", None), P(None, "gx", "gy", None)),
        check_vma=False,
    )
```
